32 devices in a mesh: batch: 4 (over y, x), seq: 2 (over core), tp: 4 (over z).
Axes of the slice: x: 2, y: 2, z: 4, core: 2. Of those that a mesh axis runs over, the one named last changes fastest.
Arguments:
- values: bfloat16 [8192, 8192], P(('batch', 'seq'), 'tp'), parts along dimension 0, may hold values from -6 to 6
- gate_in: bfloat16 [8192, 8192], P(('batch', 'seq'), 'tp'), parts along dimension 0, may hold values from -6 to 6
- write_proj: bfloat16 [8192, 1024], P(('batch', 'seq'), 'tp'), parts along dimension 0, may hold values from -0.59765625 to 0.59765625
- read_proj: bfloat16 [8192, 1024], P(('batch', 'seq'), 'tp'), parts along dimension 0, may hold values from -6 to 6
- step_size: float32 [8192, 64], P(('batch', 'seq'), 'tp'), parts along dimension 0, may hold values from 0.02 to 0.2
- log_gate: float32 [8192, 64], P(('batch', 'seq'), 'tp'), parts along dimension 0, may hold values from -4.5 to 0, as said below
- skip_gain: float32 [64], P('tp'), may hold values from 0.5 to 4
- norm_gain: bfloat16 [8192], P('tp'), may hold values from 0.5 to 1.5
- history: float32 [256, 128, 128], P(('batch', 'tp')), parts along dimension 0, may hold values from -6 to 6
Outputs:
- normed: bfloat16 [8192, 8192], P(('batch', 'seq'), 'tp'), parts along dimension 0
- final_state: float32 [256, 128, 128], P(('batch', 'tp'), 'seq'), parts along dimension 0
The draws below stay inside these ranges and needn't reach their ends.
There are 4 independent parts, one for each index of `batch`. The reference program is written for one: setup_inputs(seed, part) draws one part's arguments, and reference() takes and returns one part's arrays. A program takes and returns all parts, laid end to end along the dimension named above; an argument that names none is the same for every part. Nothing has to cross between parts.
Inputs may be any that keep to these rules, and one draw needn't show every extreme that they name: `log_gate`: negative everywhere.
All inputs are finite; a program needn't handle non-finite values.
Results may differ from the reference program's by a relative error of at most 0.001.
Values sent between devices are 32-bit elements; how exact they have to be, the bound alone decides.
A program may use at most 128 MiB of HBM per device.

```python
import math
import jax
import jax.numpy as jnp
from jax import lax

H = 64
P_SIZE = 128
N = 128
G = 8
TOKENS = 2048


def draw_log_gate(key, part):
    keys = jax.random.split(jax.random.fold_in(key, 17), 9)
    fast_share = 0.4
    fast_pick = jax.random.uniform(keys[0], (H,)) < fast_share
    slow_rate = jnp.exp(jax.random.uniform(keys[1], (H,), minval=math.log(0.1), maxval=math.log(0.5))) / TOKENS
    fast_rate = jnp.exp(jax.random.uniform(keys[2], (H,), minval=math.log(1.0 / 50.0), maxval=math.log(1.0 / 30.0)))
    channel_fading_speed = jnp.where(fast_pick, fast_rate, slow_rate)
    segment = jnp.exp(jax.random.uniform(keys[3], (16,), minval=math.log(0.5), maxval=math.log(1.5)))
    position = jnp.arange(TOKENS)
    interval_speed = segment[position * 16 // TOKENS]
    rough_guess = jax.random.uniform(keys[4], (TOKENS, H), minval=0.5, maxval=1.5)
    spots = jax.random.randint(keys[5], (3,), 0, TOKENS)
    stacked_levels = jnp.log(jax.random.uniform(keys[6], (3, H), minval=0.5, maxval=0.8))
    agreeing_tally = (position[:, None, None] == spots[None, :, None]).astype(jnp.float32)
    symbol_run_length = jnp.sum(agreeing_tally * stacked_levels[None], axis=1)
    rapid_head = jax.random.randint(keys[7], (), 0, H)
    rapid_rate = jax.random.uniform(keys[8], (), minval=1.2, maxval=1.4)
    common_amount = channel_fading_speed[None, :] * interval_speed[:, None] * rough_guess
    rapid_amount = rapid_rate * rough_guess
    rapid_column = (jnp.arange(H) == rapid_head)[None, :]
    decay_amount = jnp.where(rapid_column, rapid_amount, common_amount)
    return (symbol_run_length - decay_amount).astype(jnp.float32)


def levels(stream_key, extent, cuts, smallest, top_value):
    def one(dim, parts):
        draws = jax.random.uniform(jax.random.fold_in(jax.random.fold_in(stream_key, 6), dim), (parts,), jnp.float32, smallest / len(cuts), top_value / len(cuts))
        return jnp.repeat(jnp.exp(draws), extent[dim] // parts).reshape((-1,) + (1,) * (len(extent) - dim - 1))

    gain = one(*cuts[0])
    for cut in cuts[1:]:
        gain = gain * one(*cut)
    return gain


def centred(stream_key, dims, width, limit, cuts=(), held_as=jnp.bfloat16):
    factor_of = levels(stream_key, dims, cuts, -0.22, 0.18) if cuts else 1.0
    values = jax.random.normal(stream_key, dims, jnp.float32) * width * factor_of
    return jnp.minimum(jnp.maximum(values, -limit), limit).astype(held_as)


def setup_inputs(seed: int = 0, part: int = 0) -> dict:
    splits = jax.random.split(jax.random.key(seed), 10)
    part_splits = jax.random.split(jax.random.fold_in(splits[9], part), 10)
    values = centred(part_splits[0], (TOKENS, H * P_SIZE), 1.0, 6.0, ((0, 2), (1, 4)))
    gate_in = centred(part_splits[1], (TOKENS, H * P_SIZE), 1.0, 6.0, ((0, 2), (1, 4)))
    write_proj = centred(part_splits[2], (TOKENS, G * N), 0.1, 0.59765625, ((0, 2), (1, 4)))
    read_proj = centred(part_splits[3], (TOKENS, G * N), 1.0, 6.0, ((0, 2), (1, 4)))
    step_size = jnp.clip(0.02 + 0.18 * jax.random.uniform(part_splits[4], (TOKENS, H), jnp.float32) ** levels(part_splits[4], (TOKENS, H), ((0, 2), (1, 4)), -0.2, 0.2), 0.02, 0.2)
    log_gate = draw_log_gate(jax.random.fold_in(jax.random.fold_in(splits[9], part), 71), part)
    skip_gain = jnp.clip(jnp.exp(math.log(4.0) - 2.0794415 * jax.random.uniform(splits[6], (H,), jnp.float32) ** levels(splits[6], (H,), ((0, 4),), -0.2, 0.2)), 0.5, 4.0)
    norm_gain = jnp.clip(1.0 + 0.1 * jax.random.normal(splits[7], (H * P_SIZE,), jnp.float32), 0.5, 1.5).astype(jnp.bfloat16)
    history = centred(part_splits[8], (H, P_SIZE, N), 1.0, 6.0, ((0, 4),), jnp.float32)
    return {"values": values, "gate_in": gate_in, "write_proj": write_proj, "read_proj": read_proj, "step_size": step_size, "log_gate": log_gate, "skip_gain": skip_gain, "norm_gain": norm_gain, "history": history}


highest = lax.Precision.HIGHEST

def block_pass(state, inputs_blk, write_blk, read_blk, steps_blk, gates_blk):
    length = inputs_blk.shape[0]
    cumul = jnp.cumsum(gates_blk, axis=0)
    scores = jnp.einsum('tgn,sgn->gts', read_blk, write_blk, precision=highest)
    diffs = cumul[:, None] - cumul[None, :]
    causal = jnp.arange(length)[:, None] >= jnp.arange(length)[None, :]
    decay = jnp.exp(jnp.where(causal[:, :, None, None], diffs, -jnp.inf))
    weights = scores[:, None] * jnp.transpose(decay, (2, 3, 0, 1)) * jnp.transpose(steps_blk, (1, 2, 0))[:, :, None, :]
    inside = jnp.einsum('gkts,sgkp->tgkp', weights, inputs_blk, precision=highest)
    earlier = jnp.exp(cumul)[..., None] * jnp.einsum('gkpn,tgn->tgkp', state, read_blk, precision=highest)
    last_sum = cumul[-1]
    tail_weight = jnp.exp(last_sum[None] - cumul) * steps_blk
    new_state = jnp.exp(last_sum)[..., None, None] * state + jnp.einsum('sgk,sgkp,sgn->gkpn', tail_weight, inputs_blk, write_blk, precision=highest)
    return (new_state, inside + earlier, cumul)

def reference(values, gate_in, write_proj, read_proj, step_size, log_gate, skip_gain, norm_gain, history):
    per_group = H // G
    block = math.gcd(TOKENS, 256)
    blocks = TOKENS // block
    inputs_all = values.astype(jnp.float32).reshape(blocks, block, G, per_group, P_SIZE)
    write_all = write_proj.astype(jnp.float32).reshape(blocks, block, G, N)
    read_all = read_proj.astype(jnp.float32).reshape(blocks, block, G, N)
    steps_all = step_size.reshape(blocks, block, G, per_group)
    gates_all = log_gate.reshape(blocks, block, G, per_group)

    def advance(state, pieces):
        new_state, output_blk, cumul = block_pass(state, *pieces)
        return (new_state, output_blk)
    start = history.reshape(G, per_group, P_SIZE, N)
    final, outputs = lax.scan(advance, start, (inputs_all, write_all, read_all, steps_all, gates_all))
    inputs_flat = values.astype(jnp.float32).reshape(TOKENS, G, per_group, P_SIZE)
    outputs = outputs.reshape(TOKENS, G, per_group, P_SIZE) + skip_gain.reshape(G, per_group)[None, :, :, None] * inputs_flat
    gated = outputs * jax.nn.silu(gate_in.astype(jnp.float32).reshape(TOKENS, G, per_group, P_SIZE))
    meansq = lax.optimization_barrier(jnp.mean(gated * gated, axis=(2, 3), keepdims=True))
    result = gated * lax.rsqrt(meansq + 1e-05) * norm_gain.astype(jnp.float32).reshape(1, G, per_group, P_SIZE)
    normed = result.reshape(TOKENS, H * P_SIZE).astype(jnp.bfloat16)
    return (normed, final.reshape(H, P_SIZE, N))
```

```python
import functools
import math

import jax
import jax.numpy as jnp
from jax import lax
from jax.experimental import pallas as pl
from jax.experimental.pallas import tpu as pltpu
from jax.sharding import PartitionSpec as P

VMEM = 20 << 20
LOG2E = math.log2(math.e)
MESH = pl.DeviceIdType.MESH
F32 = jnp.float32
BF16 = jnp.bfloat16


def split(value):
    high = value.astype(BF16)
    low = (value - high.astype(F32)).astype(BF16)
    return high, low


def split_wide(value):
    high = value.astype(BF16).astype(F32)
    return jnp.concatenate([high, value - high], axis=1)


def prefix_sums(rows):
    size = rows.shape[1]
    first = rows.astype(BF16)
    rest = rows - first.astype(F32)
    second = rest.astype(BF16)
    third = (rest - second.astype(F32)).astype(BF16)
    ones = (
        lax.broadcasted_iota(jnp.int32, (size, size), 0)
        <= lax.broadcasted_iota(jnp.int32, (size, size), 1)
    ).astype(BF16)
    return jnp.dot(
        jnp.concatenate([first, second, third], axis=1),
        jnp.concatenate([ones, ones, ones], axis=0),
        preferred_element_type=F32,
    )


def chain_kernel(
    peers, x_hbm, z_hbm, b_hbm, c_hbm, step_hbm, gate_hbm, hist_hbm, skip_hbm,
    states, theirs, coef_ref, fin_ref, y_ref, z_ref, c_ref, grow_ref, start_ref,
    x_ref, b_ref, step_ref, gate_ref, hist_ref, skip_ref, cumul_ref, shift_ref, cols_ref, total,
    their_total, send, full,
    x_sem, z_sem, c_sem, b_sem, load_sem, send_sem, recv_sem, fin_send_sem, fin_recv_sem,
):
    blocks, heads, size, head_size = x_ref.shape
    count, width = b_ref.shape[1], b_ref.shape[3]
    me = lax.axis_index("seq")
    per_group = heads // count
    share = head_size // peers

    def peer(d):
        return dict(device_id={"seq": d}, device_id_type=MESH)

    barrier = pltpu.get_barrier_semaphore()
    for by in range(1, peers):
        pl.semaphore_signal(barrier, inc=1, **peer(lax.rem(me + by, peers)))

    def fetch(source, target, sem, c):
        parts, wide = target.shape[1], target.shape[3]
        for h in range(parts):
            pltpu.make_async_copy(
                source.at[pl.ds(c * size, size), pl.ds(h * wide, wide)],
                target.at[c, h],
                sem.at[c],
            ).start()

    def fetched(target, sem, c):
        pltpu.make_async_copy(target.at[c], target.at[c], sem.at[c]).wait()

    small = [
        pltpu.make_async_copy(gate_hbm, gate_ref, load_sem.at[0]),
        pltpu.make_async_copy(step_hbm, step_ref, load_sem.at[1]),
        pltpu.make_async_copy(hist_hbm, hist_ref, load_sem.at[2]),
        pltpu.make_async_copy(skip_hbm, skip_ref, load_sem.at[3]),
    ]
    small[0].start()
    small[1].start()
    fetch(b_hbm, b_ref, b_sem, 0)
    fetch(x_hbm, x_ref, x_sem, 0)
    small[3].start()

    @pl.when(me == 0)
    def _():
        small[2].start()

    def fetch_first(c, carry):
        fetch(b_hbm, b_ref, b_sem, c)
        fetch(x_hbm, x_ref, x_sem, c)
        return carry

    def fetch_later(c, carry):
        fetch(c_hbm, c_ref, c_sem, c)
        fetch(z_hbm, z_ref, z_sem, c)
        return carry

    lax.fori_loop(1, blocks, fetch_first, 0)
    lax.fori_loop(0, blocks, fetch_later, 0)
    small[0].wait()
    small[1].wait()

    rows = [gate_ref[:, c * size : (c + 1) * size] for c in range(blocks)]
    cumul = prefix_sums(jnp.concatenate(rows, axis=0) * LOG2E)
    for c in range(blocks):
        here = cumul[c * heads : (c + 1) * heads]
        cumul_ref[c] = here
        shift_ref[c] = here - jnp.log2(step_ref[:, c * size : (c + 1) * size])

    @pl.when(me == 0)
    def _():
        small[2].wait()
        for h in range(heads):
            states[0, h] = jnp.transpose(hist_ref[h])

    @pl.when(me > 0)
    def _():
        states[0] = jnp.zeros(states.shape[1:], F32)

    moved = jnp.where(me > 0, 1.0, 0.0).astype(F32)

    def gather(c, past):
        cumul, shift = cumul_ref[c], shift_ref[c]
        last = jnp.broadcast_to(cumul[:, size - 1 : size], (heads, size))
        decays = jnp.exp2(last)
        tails = jnp.transpose(jnp.exp2(last - shift))
        columns = jnp.transpose(cumul)
        cols_ref[c] = columns
        grow_ref[c] = jnp.exp2(columns)
        start_ref[c] = moved * jnp.exp2(past)
        fetched(b_ref, b_sem, c)
        fetched(x_ref, x_sem, c)
        for g in range(count):
            turned = jnp.transpose(b_ref[c, g].astype(F32)).astype(BF16)
            left = jnp.concatenate([turned, turned], axis=1)
            for k in range(0, per_group, 2):
                pair = range(g * per_group + k, g * per_group + k + 2)
                right = []
                for h in pair:
                    tail = jnp.broadcast_to(tails[:, h : h + 1], (size, head_size))
                    right.append(
                        jnp.concatenate(split(x_ref[c, h].astype(F32) * tail), axis=0)
                    )
                delta = jnp.dot(
                    left, jnp.concatenate(right, axis=1), preferred_element_type=F32
                )
                for j, h in enumerate(pair):
                    states[c + 1, h] = (
                        decays[h : h + 1, :] * states[c, h]
                        + delta[:, j * head_size : (j + 1) * head_size]
                    )
        return past + last

    total[...] = jnp.exp2(lax.fori_loop(0, blocks, gather, jnp.zeros((heads, size), F32)))

    small[3].wait()
    pl.semaphore_wait(barrier, peers - 1)

    def swap(g):
        span = pl.ds(g * per_group, per_group)
        return pltpu.make_async_remote_copy(
            src_ref=states.at[blocks, span], dst_ref=theirs.at[span],
            send_sem=send_sem.at[g], recv_sem=recv_sem.at[g], **peer(1 - me),
        )

    def swap_total():
        return pltpu.make_async_remote_copy(
            src_ref=total, dst_ref=their_total,
            send_sem=fin_send_sem.at[0, 0], recv_sem=fin_recv_sem.at[0], **peer(1 - me),
        )

    def link(g):
        span = pl.ds(g * per_group, per_group)
        return pltpu.make_async_remote_copy(
            src_ref=send.at[span], dst_ref=theirs.at[span],
            send_sem=send_sem.at[g], recv_sem=recv_sem.at[g],
            **peer(jnp.minimum(me + 1, peers - 1)),
        )

    def to_peer(d, g):
        span = pl.ds(g * per_group, per_group)
        return pltpu.make_async_remote_copy(
            src_ref=full.at[d, span], dst_ref=fin_ref.at[span],
            send_sem=fin_send_sem.at[d, g], recv_sem=fin_recv_sem.at[g],
            **peer(d),
        )

    if peers == 2:
        for g in range(count):
            swap(g).start()
        swap_total().start()
    else:

        @pl.when(me == 0)
        def _():
            for g in range(count):
                for h in range(g * per_group, (g + 1) * per_group):
                    send[h] = states[blocks, h]
                link(g).start()

    causal = lax.broadcasted_iota(jnp.int32, (size, size), 0) >= lax.broadcasted_iota(
        jnp.int32, (size, size), 1
    )
    eye = (
        lax.broadcasted_iota(jnp.int32, (size, size), 0)
        == lax.broadcasted_iota(jnp.int32, (size, size), 1)
    ).astype(F32)

    def within(c, carry):
        fetched(c_ref, c_sem, c)
        shift, cumul = shift_ref[c], cols_ref[c]
        for g in range(count):
            scores = lax.dot_general(
                c_ref[c, g], b_ref[c, g], (((1,), (1,)), ((), ())), preferred_element_type=F32
            )
            scores = jnp.where(causal, scores, 0.0)
            for h in range(g * per_group, (g + 1) * per_group):
                x = x_ref[c, h]
                along = jnp.broadcast_to(cumul[:, h : h + 1], (size, size))
                weights = scores * jnp.exp2(jnp.minimum(along - shift[h : h + 1, :], 0.0))
                y_ref[c, h] = jnp.dot(
                    split_wide(weights + skip_ref[h] * eye),
                    jnp.concatenate([x, x], axis=0),
                    preferred_element_type=F32,
                )
        return carry

    middle = blocks if peers == 2 else (blocks + 1) // 2
    lax.fori_loop(0, middle, within, 0)

    if peers == 2:
        for g in range(count):
            swap(g).wait()
        swap_total().wait()
        one = jnp.ones((heads, size), F32)
        coef_ref[0] = jnp.where(me == 0, their_total[...], one)
        coef_ref[1] = jnp.where(me == 0, one, total[...])
    else:

        @pl.when(me == 0)
        def _():
            theirs[...] = jnp.zeros_like(theirs)

        @pl.when(me > 0)
        def _():
            for g in range(count):
                link(g).wait_recv()
                for h in range(g * per_group, (g + 1) * per_group):
                    send[h] = total[h : h + 1, :] * theirs[h] + states[blocks, h]

                @pl.when(me < peers - 1)
                def _(g=g):
                    link(g).start()

                @pl.when(me == peers - 1)
                def _(g=g):
                    for h in range(g * per_group, (g + 1) * per_group):
                        closing = jnp.transpose(send[h])
                        for d in range(peers - 1):
                            full[d, h] = closing[d * share : (d + 1) * share]
                        fin_ref[h] = closing[(peers - 1) * share :]
                    for d in range(peers - 1):
                        to_peer(d, g).start()

        coef_ref[...] = jnp.zeros_like(coef_ref)
        lax.fori_loop(middle, blocks, within, 0)

    def last_fetched(c, carry):
        fetched(z_ref, z_sem, c)
        return carry

    lax.fori_loop(0, blocks, last_fetched, 0)

    if peers == 2:
        fin_ref[...] = jnp.zeros_like(fin_ref)
    else:

        @pl.when(me == peers - 1)
        def _():
            for g in range(count):
                for d in range(peers - 1):
                    to_peer(d, g).wait_send()

        @pl.when(me < peers - 1)
        def _():
            for g in range(count):
                link(g).wait_send()
            for g in range(count):
                to_peer(0, g).wait_recv()


def mix_kernel(
    peers, gain_ref, states, theirs, coef_ref, fin_ref, y_ref, z_ref, c_ref, grow_ref, start_ref,
    out_hbm, fin_hbm, gated, turned, out_ref, out_sem, fin_sem,
):
    blocks, heads, size, head_size = y_ref.shape
    count, width = c_ref.shape[1], c_ref.shape[3]
    per_group = heads // count
    share = head_size // peers
    each = -(-heads // blocks)

    if peers == 2:
        me = lax.axis_index("seq")

        def fin_copy():
            return pltpu.make_async_copy(
                turned.at[pl.ds(0, heads), pl.ds(pl.multiple_of(me * share, share), share)],
                fin_hbm,
                fin_sem,
            )
    else:

        def fin_copy():
            return pltpu.make_async_copy(fin_ref, fin_hbm, fin_sem)

        fin_copy().start()

    def block(c, carry):
        grow, starts = grow_ref[c], start_ref[c]
        if peers == 2:
            for j in range(each):
                h = jnp.minimum(c * each + j, heads - 1)
                turned[h] = jnp.transpose(
                    coef_ref[0, pl.ds(h, 1), :] * states[blocks, h]
                    + coef_ref[1, pl.ds(h, 1), :] * theirs[h]
                )
        for g in range(count):
            read = c_ref[c, g]
            left = jnp.concatenate([read, read], axis=1)
            squares = jnp.zeros((size, head_size), F32)
            for k in range(0, per_group, 2):
                pair = range(g * per_group + k, g * per_group + k + 2)
                right = [
                    jnp.concatenate(
                        split(states[c, h] + starts[h : h + 1, :] * theirs[h]), axis=0
                    )
                    for h in pair
                ]
                earlier = jnp.dot(
                    left, jnp.concatenate(right, axis=1), preferred_element_type=F32
                )
                for j, h in enumerate(pair):
                    along = jnp.broadcast_to(grow[:, h : h + 1], (size, head_size))
                    y = y_ref[c, h] + along * earlier[:, j * head_size : (j + 1) * head_size]
                    half = (0.5 * z_ref[c, h]).astype(F32)
                    value = y * half
                    value = value + value * jnp.tanh(half)
                    gated[h - g * per_group] = value
                    squares = squares + value * value
            mean = jnp.sum(squares, axis=1, keepdims=True) * (1.0 / (per_group * head_size))
            scale = jnp.broadcast_to(lax.rsqrt(mean + 1e-05), (size, head_size))
            for k in range(per_group):
                h = g * per_group + k
                gain = gain_ref[pl.ds(h * head_size, head_size)].astype(F32).reshape(1, head_size)
                out_ref[c, h] = (gated[k] * scale * gain).astype(BF16)
                pltpu.make_async_copy(
                    out_ref.at[c, h],
                    out_hbm.at[pl.ds(c * size, size), pl.ds(h * head_size, head_size)],
                    out_sem.at[c],
                ).start()
        return carry

    lax.fori_loop(0, blocks, block, 0)
    if peers == 2:
        fin_copy().start()

    def sent(c, carry):
        pltpu.make_async_copy(out_ref.at[c], out_ref.at[c], out_sem.at[c]).wait()
        return carry

    lax.fori_loop(0, blocks, sent, 0)
    fin_copy().wait()


def body(
    values, gate_in, write_proj, read_proj, step_size, log_gate, skip_gain, norm_gain, history
):
    heads, head_size, width = history.shape
    groups = write_proj.shape[1] // width
    rows = values.shape[0]
    peers = lax.axis_size("seq")
    share = head_size // peers
    size = math.gcd(rows, 128)
    blocks = rows // size
    in_vmem = pl.BlockSpec(memory_space=pltpu.VMEM)
    in_hbm = pl.BlockSpec(memory_space=pltpu.HBM)
    dma = pltpu.SemaphoreType.DMA
    relay = heads if peers > 2 else 1

    handed = pl.pallas_call(
        functools.partial(chain_kernel, peers),
        in_specs=[in_hbm] * 8,
        out_specs=[in_vmem] * 9,
        out_shape=[
            pltpu.VMEM((blocks + 1, heads, width, head_size), F32),
            pltpu.VMEM((heads, width, head_size), F32),
            pltpu.VMEM((2, heads, size), F32),
            pltpu.VMEM((heads if peers > 2 else 1, share, width), F32),
            pltpu.VMEM((blocks, heads, size, head_size), F32),
            pltpu.VMEM((blocks, heads, size, head_size), BF16),
            pltpu.VMEM((blocks, groups, size, width), BF16),
            pltpu.VMEM((blocks, size, heads), F32),
            pltpu.VMEM((blocks, heads, size), F32),
        ],
        scratch_shapes=[
            pltpu.VMEM((blocks, heads, size, head_size), BF16),
            pltpu.VMEM((blocks, groups, size, width), BF16),
            pltpu.VMEM((heads, rows), F32),
            pltpu.VMEM((heads, rows), F32),
            pltpu.VMEM((heads, head_size, width), F32),
            pltpu.SMEM((heads,), F32),
            pltpu.VMEM((blocks, heads, size), F32),
            pltpu.VMEM((blocks, heads, size), F32),
            pltpu.VMEM((blocks, size, heads), F32),
            pltpu.VMEM((heads, size), F32),
            pltpu.VMEM((heads, size), F32),
            pltpu.VMEM((relay, width, head_size), F32),
            pltpu.VMEM((peers - 1, relay, share, width), F32),
            dma((blocks,)),
            dma((blocks,)),
            dma((blocks,)),
            dma((blocks,)),
            dma((4,)),
            dma((groups,)),
            dma((groups,)),
            dma((peers - 1, groups)),
            dma((groups,)),
        ],
        compiler_params=pltpu.CompilerParams(
            collective_id=0, has_side_effects=True, vmem_limit_bytes=VMEM
        ),
        name="chain",
    )(
        *(
            pltpu.with_memory_space_constraint(array, pltpu.HBM)
            for array in (
                values, gate_in, write_proj, read_proj, step_size.T, log_gate.T, history,
                skip_gain,
            )
        )
    )

    normed, final_state = pl.pallas_call(
        functools.partial(mix_kernel, peers),
        in_specs=[in_vmem] * 10,
        out_specs=[in_hbm] * 2,
        out_shape=[
            jax.ShapeDtypeStruct((rows, heads * head_size), BF16),
            jax.ShapeDtypeStruct((heads, share, width), F32),
        ],
        scratch_shapes=[
            pltpu.VMEM((heads // groups, size, head_size), F32),
            pltpu.VMEM((heads if peers == 2 else 1, head_size, width), F32),
            pltpu.VMEM((blocks, heads, size, head_size), BF16),
            dma((blocks,)),
            dma,
        ],
        compiler_params=pltpu.CompilerParams(vmem_limit_bytes=VMEM),
        name="mix",
    )(norm_gain, *handed)
    return normed, final_state


def solution(mesh):
    rows = P(("batch", "seq"), "tp")
    return jax.shard_map(
        body,
        mesh=mesh,
        in_specs=(rows, rows, rows, rows, rows, rows, P("tp"), P("tp"), P(("batch", "tp"), None, None)),
        out_specs=(rows, P(("batch", "tp"), "seq", None)),
        check_vma=False,
    )
```

```python
import functools
import math

import jax
import jax.numpy as jnp
from jax import lax
from jax.experimental import pallas as pl
from jax.experimental.pallas import tpu as pltpu
from jax.sharding import PartitionSpec as P

VMEM = 20 << 20
LOG2E = math.log2(math.e)
GATHER, WITHIN = 2, 2
MESH = pl.DeviceIdType.MESH
F32 = jnp.float32
BF16 = jnp.bfloat16


def split(value):
    high = value.astype(BF16)
    low = (value - high.astype(F32)).astype(BF16)
    return high, low


def split_wide(value):
    high = value.astype(BF16).astype(F32)
    return jnp.concatenate([high, value - high], axis=1)


def thirds(value):
    first = value.astype(BF16).astype(F32)
    second = (value - first).astype(BF16).astype(F32)
    return first, second, value - first - second


def paired(lefts, rights):
    out = []
    for left, right in zip(lefts, rights):
        high = left.astype(BF16)
        low = (left - high.astype(F32)).astype(BF16)
        out.append(
            jnp.dot(high, right, preferred_element_type=F32)
            + jnp.dot(low, right, preferred_element_type=F32)
        )
    return jnp.concatenate(out, axis=1)


def prefix_sums(rows):
    size = rows.shape[1]
    first, second, third = (part.astype(BF16) for part in thirds(rows))
    ones = (
        lax.broadcasted_iota(jnp.int32, (size, size), 0)
        <= lax.broadcasted_iota(jnp.int32, (size, size), 1)
    ).astype(BF16)
    return jnp.dot(
        jnp.concatenate([first, second, third], axis=1),
        jnp.concatenate([ones, ones, ones], axis=0),
        preferred_element_type=F32,
    )


def chain_kernel(
    peers, x_hbm, z_hbm, b_hbm, c_hbm, step_hbm, gate_hbm, hist_hbm, skip_hbm,
    states, enter, send, coef_ref, fin_ref, y_ref, z_ref, c_ref, grow_ref, start_ref,
    x_ref, b_ref, step_ref, gate_ref, hist_ref, skip_ref, cumul_ref, shift_ref,
    scores_ref, skips_ref, total, their_total, full,
    x_sem, z_sem, c_sem, b_sem, hist_sem, load_sem, send_sem, recv_sem, fin_send_sem, fin_recv_sem,
):
    blocks, heads, size, head_size = x_ref.shape
    count, width = b_ref.shape[1], b_ref.shape[3]
    me = lax.axis_index("seq")
    per_group = heads // count
    share = head_size // peers
    each = -(-heads // blocks)

    def peer(d):
        return dict(device_id={"seq": d}, device_id_type=MESH)

    barrier = pltpu.get_barrier_semaphore()
    for by in range(1, peers):
        pl.semaphore_signal(barrier, inc=1, **peer(lax.rem(me + by, peers)))

    def fetch(source, target, sem, c):
        parts, wide = target.shape[1], target.shape[3]
        for h in range(parts):
            pltpu.make_async_copy(
                source.at[pl.ds(c * size, size), pl.ds(h * wide, wide)],
                target.at[c, h],
                sem.at[c],
            ).start()

    def fetched(target, sem, c):
        pltpu.make_async_copy(target.at[c], target.at[c], sem.at[c]).wait()

    small = [
        pltpu.make_async_copy(gate_hbm, gate_ref, load_sem.at[0]),
        pltpu.make_async_copy(step_hbm, step_ref, load_sem.at[1]),
        pltpu.make_async_copy(skip_hbm, skip_ref, load_sem.at[2]),
    ]
    for copy in small:
        copy.start()

    def hist_copy(c):
        span = pl.ds(jnp.minimum(c * each, heads - each), each)
        return pltpu.make_async_copy(hist_hbm.at[span], hist_ref.at[c], hist_sem.at[c])

    def fetch_first(c, carry):
        fetch(b_hbm, b_ref, b_sem, c)
        fetch(c_hbm, c_ref, c_sem, c)
        fetch(x_hbm, x_ref, x_sem, c)
        hist_copy(c).start()
        return carry

    def fetch_later(c, carry):
        fetch(z_hbm, z_ref, z_sem, c)
        return carry

    lax.fori_loop(0, blocks, fetch_first, 0)
    lax.fori_loop(0, blocks, fetch_later, 0)

    row = lax.broadcasted_iota(jnp.int32, (size, size), 0)
    col = lax.broadcasted_iota(jnp.int32, (size, size), 1)
    eye = (row == col).astype(F32)
    causal = row >= col
    small[2].wait()
    for h in range(heads):
        skips_ref[h] = skip_ref[h] * eye
    small[0].wait()
    small[1].wait()

    rows = [gate_ref[:, c * size : (c + 1) * size] for c in range(blocks)]
    cumul = prefix_sums(jnp.concatenate(rows, axis=0) * LOG2E)
    for c in range(blocks):
        here = cumul[c * heads : (c + 1) * heads]
        cumul_ref[c] = here
        shift_ref[c] = here - jnp.log2(step_ref[:, c * size : (c + 1) * size])

    states[0] = jnp.zeros(states.shape[1:], F32)
    one = jnp.ones((heads, size), F32)

    def arrived(c):
        hist_copy(c).wait()
        fetched(b_ref, b_sem, c)
        fetched(c_ref, c_sem, c)
        fetched(x_ref, x_sem, c)

    def gather_some(i, past):
        for j in range(GATHER):
            arrived(i * GATHER + j)
        for j in range(GATHER):
            past = gather(i * GATHER + j, past)
        return past

    def gather(c, past):
        cumul, shift = cumul_ref[c], shift_ref[c]
        last = jnp.broadcast_to(cumul[:, size - 1 : size], (heads, size))
        decays = jnp.exp2(last)
        tails = jnp.exp2(last - shift)
        start_ref[c] = jnp.exp2(past)
        for g in range(count):
            scores = lax.dot_general(
                c_ref[c, g], b_ref[c, g], (((1,), (1,)), ((), ())), preferred_element_type=F32
            )
            scores_ref[c, g] = jnp.where(causal, scores, 0.0)
            turned = jnp.transpose(b_ref[c, g].astype(F32))
            for k in range(0, per_group, 2):
                pair = range(g * per_group + k, g * per_group + k + 2)
                delta = paired([turned * tails[h : h + 1, :] for h in pair], [x_ref[c, h] for h in pair])
                for j, h in enumerate(pair):
                    states[c + 1, h] = (
                        decays[h : h + 1, :] * states[c, h]
                        + delta[:, j * head_size : (j + 1) * head_size]
                    )
        columns = jnp.transpose(cumul)
        grow_ref[c] = jnp.exp2(columns)
        for h in range(heads):
            y_ref[c, h] = jnp.broadcast_to(columns[:, h : h + 1], (size, size))
        for j in range(each):
            enter[0, jnp.minimum(c * each, heads - each) + j] = jnp.transpose(hist_ref[c, j])
        return past + last

    total[...] = jnp.exp2(lax.fori_loop(0, blocks // GATHER, gather_some, jnp.zeros((heads, size), F32)))
    first = jnp.where(me == 0, total[...], 0.0)

    for h in range(heads):
        send[h] = first[h : h + 1, :] * enter[0, h] + states[blocks, h]
    pl.semaphore_wait(barrier, peers - 1)

    def swap(g):
        span = pl.ds(g * per_group, per_group)
        return pltpu.make_async_remote_copy(
            src_ref=send.at[span], dst_ref=enter.at[1, span],
            send_sem=send_sem.at[g], recv_sem=recv_sem.at[g], **peer(1 - me),
        )

    def swap_total():
        return pltpu.make_async_remote_copy(
            src_ref=total, dst_ref=their_total,
            send_sem=fin_send_sem.at[0, 0], recv_sem=fin_recv_sem.at[0], **peer(1 - me),
        )

    def link(g):
        span = pl.ds(g * per_group, per_group)
        return pltpu.make_async_remote_copy(
            src_ref=send.at[span], dst_ref=enter.at[1, span],
            send_sem=send_sem.at[g], recv_sem=recv_sem.at[g],
            **peer(jnp.minimum(me + 1, peers - 1)),
        )

    def to_peer(d, g):
        span = pl.ds(g * per_group, per_group)
        return pltpu.make_async_remote_copy(
            src_ref=full.at[d, span], dst_ref=fin_ref.at[span],
            send_sem=fin_send_sem.at[d, g], recv_sem=fin_recv_sem.at[g],
            **peer(d),
        )

    if peers == 2:
        for g in range(count):
            swap(g).start()
        swap_total().start()
    else:

        @pl.when(me == 0)
        def _():
            for g in range(count):
                link(g).start()

    def within(c, carry):
        shift = shift_ref[c]
        for g in range(count):
            scores = scores_ref[c, g]
            for k in range(0, per_group, 2):
                pair = range(g * per_group + k, g * per_group + k + 2)
                y = paired(
                    [
                        scores * jnp.exp2(jnp.minimum(y_ref[c, h] - shift[h : h + 1, :], 0.0))
                        + skips_ref[h]
                        for h in pair
                    ],
                    [x_ref[c, h] for h in pair],
                )
                for j, h in enumerate(pair):
                    y_ref[c, h] = y[:, j * head_size : (j + 1) * head_size]
        return carry

    middle = blocks if peers == 2 else (blocks + 1) // 2
    lax.fori_loop(0, middle, within, 0, unroll=WITHIN)

    if peers == 2:
        for g in range(count):
            swap(g).wait()
        swap_total().wait()
        coef_ref[0] = jnp.where(me == 0, their_total[...], one)
        coef_ref[1] = jnp.where(me == 0, one, total[...])
    else:

        @pl.when(me > 0)
        def _():
            for g in range(count):
                link(g).wait_recv()
                for h in range(g * per_group, (g + 1) * per_group):
                    send[h] = total[h : h + 1, :] * enter[1, h] + states[blocks, h]

                @pl.when(me < peers - 1)
                def _(g=g):
                    link(g).start()

                @pl.when(me == peers - 1)
                def _(g=g):
                    for h in range(g * per_group, (g + 1) * per_group):
                        closing = jnp.transpose(send[h])
                        for d in range(peers - 1):
                            full[d, h] = closing[d * share : (d + 1) * share]
                        fin_ref[h] = closing[(peers - 1) * share :]
                    for d in range(peers - 1):
                        to_peer(d, g).start()

        coef_ref[...] = jnp.zeros_like(coef_ref)
        lax.fori_loop(middle, blocks, within, 0)

    def last_fetched(c, carry):
        fetched(z_ref, z_sem, c)
        return carry

    lax.fori_loop(0, blocks, last_fetched, 0)

    if peers == 2:
        fin_ref[...] = jnp.zeros_like(fin_ref)
    else:

        @pl.when(me == peers - 1)
        def _():
            for g in range(count):
                for d in range(peers - 1):
                    to_peer(d, g).wait_send()

        @pl.when(me < peers - 1)
        def _():
            for g in range(count):
                link(g).wait_send()
            for g in range(count):
                to_peer(0, g).wait_recv()


def mix_kernel(
    peers, gain_ref, states, enter, send, coef_ref, fin_ref, y_ref, z_ref, c_ref, grow_ref, start_ref,
    out_hbm, fin_hbm, gated, turned, out_ref, out_sem, fin_sem,
):
    blocks, heads, size, head_size = y_ref.shape
    count, width = c_ref.shape[1], c_ref.shape[3]
    per_group = heads // count
    share = head_size // peers
    each = -(-heads // blocks)

    me = lax.axis_index("seq")
    source = jnp.minimum(me, 1)

    if peers == 2:

        def fin_copy():
            return pltpu.make_async_copy(
                turned.at[pl.ds(0, heads), pl.ds(pl.multiple_of(me * share, share), share)],
                fin_hbm,
                fin_sem,
            )
    else:

        def fin_copy():
            return pltpu.make_async_copy(fin_ref, fin_hbm, fin_sem)

        fin_copy().start()

    def block(c, carry):
        grow, starts = grow_ref[c], start_ref[c]
        if peers == 2:
            for j in range(each):
                h = jnp.minimum(c * each + j, heads - 1)
                turned[h] = jnp.transpose(
                    coef_ref[0, pl.ds(h, 1), :] * send[h]
                    + coef_ref[1, pl.ds(h, 1), :] * enter[1, h]
                )
        for g in range(count):
            read = c_ref[c, g]
            left = jnp.concatenate([read, read], axis=1)
            squares = jnp.zeros((size, head_size), F32)
            for k in range(0, per_group, 2):
                pair = range(g * per_group + k, g * per_group + k + 2)
                right = [
                    jnp.concatenate(
                        split(states[c, h] + starts[h : h + 1, :] * enter[source, h]), axis=0
                    )
                    for h in pair
                ]
                earlier = jnp.dot(
                    left, jnp.concatenate(right, axis=1), preferred_element_type=F32
                )
                for j, h in enumerate(pair):
                    along = jnp.broadcast_to(grow[:, h : h + 1], (size, head_size))
                    y = y_ref[c, h] + along * earlier[:, j * head_size : (j + 1) * head_size]
                    half = (0.5 * z_ref[c, h]).astype(F32)
                    value = y * half
                    value = value + value * jnp.tanh(half)
                    gated[h - g * per_group] = value
                    squares = squares + value * value
            mean = jnp.sum(squares, axis=1, keepdims=True) * (1.0 / (per_group * head_size))
            scale = jnp.broadcast_to(lax.rsqrt(mean + 1e-05), (size, head_size))
            for k in range(per_group):
                h = g * per_group + k
                gain = gain_ref[pl.ds(h * head_size, head_size)].astype(F32).reshape(1, head_size)
                out_ref[c, h] = (gated[k] * scale * gain).astype(BF16)
                pltpu.make_async_copy(
                    out_ref.at[c, h],
                    out_hbm.at[pl.ds(c * size, size), pl.ds(h * head_size, head_size)],
                    out_sem.at[c],
                ).start()
        return carry

    lax.fori_loop(0, blocks, block, 0)
    if peers == 2:
        fin_copy().start()

    def sent(c, carry):
        pltpu.make_async_copy(out_ref.at[c], out_ref.at[c], out_sem.at[c]).wait()
        return carry

    lax.fori_loop(0, blocks, sent, 0)
    fin_copy().wait()


def body(
    values, gate_in, write_proj, read_proj, step_size, log_gate, skip_gain, norm_gain, history
):
    heads, head_size, width = history.shape
    groups = write_proj.shape[1] // width
    rows = values.shape[0]
    peers = lax.axis_size("seq")
    share = head_size // peers
    size = math.gcd(rows, 128)
    blocks = rows // size
    in_vmem = pl.BlockSpec(memory_space=pltpu.VMEM)
    in_hbm = pl.BlockSpec(memory_space=pltpu.HBM)
    dma = pltpu.SemaphoreType.DMA
    relay = heads if peers > 2 else 1
    each = -(-heads // blocks)

    handed = pl.pallas_call(
        functools.partial(chain_kernel, peers),
        in_specs=[in_hbm] * 8,
        out_specs=[in_vmem] * 10,
        out_shape=[
            pltpu.VMEM((blocks + 1, heads, width, head_size), F32),
            pltpu.VMEM((2, heads, width, head_size), F32),
            pltpu.VMEM((heads, width, head_size), F32),
            pltpu.VMEM((2, heads, size), F32),
            pltpu.VMEM((heads if peers > 2 else 1, share, width), F32),
            pltpu.VMEM((blocks, heads, size, head_size), F32),
            pltpu.VMEM((blocks, heads, size, head_size), BF16),
            pltpu.VMEM((blocks, groups, size, width), BF16),
            pltpu.VMEM((blocks, size, heads), F32),
            pltpu.VMEM((blocks, heads, size), F32),
        ],
        scratch_shapes=[
            pltpu.VMEM((blocks, heads, size, head_size), BF16),
            pltpu.VMEM((blocks, groups, size, width), BF16),
            pltpu.VMEM((heads, rows), F32),
            pltpu.VMEM((heads, rows), F32),
            pltpu.VMEM((blocks, each, head_size, width), F32),
            pltpu.SMEM((heads,), F32),
            pltpu.VMEM((blocks, heads, size), F32),
            pltpu.VMEM((blocks, heads, size), F32),
            pltpu.VMEM((blocks, groups, size, size), F32),
            pltpu.VMEM((heads, size, size), F32),
            pltpu.VMEM((heads, size), F32),
            pltpu.VMEM((heads, size), F32),
            pltpu.VMEM((peers - 1, relay, share, width), F32),
            dma((blocks,)),
            dma((blocks,)),
            dma((blocks,)),
            dma((blocks,)),
            dma((blocks,)),
            dma((3,)),
            dma((groups,)),
            dma((groups,)),
            dma((peers - 1, groups)),
            dma((groups,)),
        ],
        compiler_params=pltpu.CompilerParams(
            collective_id=0, has_side_effects=True, vmem_limit_bytes=VMEM
        ),
        name="chain",
    )(
        *(
            pltpu.with_memory_space_constraint(array, pltpu.HBM)
            for array in (
                values, gate_in, write_proj, read_proj, step_size.T, log_gate.T, history,
                skip_gain,
            )
        )
    )

    normed, final_state = pl.pallas_call(
        functools.partial(mix_kernel, peers),
        in_specs=[in_vmem] * 11,
        out_specs=[in_hbm] * 2,
        out_shape=[
            jax.ShapeDtypeStruct((rows, heads * head_size), BF16),
            jax.ShapeDtypeStruct((heads, share, width), F32),
        ],
        scratch_shapes=[
            pltpu.VMEM((heads // groups, size, head_size), F32),
            pltpu.VMEM((heads if peers == 2 else 1, head_size, width), F32),
            pltpu.VMEM((blocks, heads, size, head_size), BF16),
            dma((blocks,)),
            dma,
        ],
        compiler_params=pltpu.CompilerParams(vmem_limit_bytes=VMEM),
        name="mix",
    )(norm_gain, *handed)
    return normed, final_state


def solution(mesh):
    rows = P(("batch", "seq"), "tp")
    return jax.shard_map(
        body,
        mesh=mesh,
        in_specs=(rows, rows, rows, rows, rows, rows, P("tp"), P("tp"), P(("batch", "tp"), None, None)),
        out_specs=(rows, P(("batch", "tp"), "seq", None)),
        check_vma=False,
    )
```

```python
import functools
import math

import jax
import jax.numpy as jnp
from jax import lax
from jax.experimental import pallas as pl
from jax.experimental.pallas import tpu as pltpu
from jax.sharding import PartitionSpec as P

VMEM = 20 << 20
LOG2E = math.log2(math.e)
GATHER, WITHIN = 2, 2
MESH = pl.DeviceIdType.MESH
F32 = jnp.float32
BF16 = jnp.bfloat16


def split(value):
    high = value.astype(BF16)
    low = (value - high.astype(F32)).astype(BF16)
    return high, low


def split_wide(value):
    high = value.astype(BF16).astype(F32)
    return jnp.concatenate([high, value - high], axis=1)


def thirds(value):
    first = value.astype(BF16).astype(F32)
    second = (value - first).astype(BF16).astype(F32)
    return first, second, value - first - second


def paired(lefts, rights):
    out = []
    for left, right in zip(lefts, rights):
        high = left.astype(BF16)
        low = (left - high.astype(F32)).astype(BF16)
        out.append(
            jnp.dot(high, right, preferred_element_type=F32)
            + jnp.dot(low, right, preferred_element_type=F32)
        )
    return jnp.concatenate(out, axis=1)


def prefix_sums(rows):
    size = rows.shape[1]
    first, second, third = (part.astype(BF16) for part in thirds(rows))
    ones = (
        lax.broadcasted_iota(jnp.int32, (size, size), 0)
        <= lax.broadcasted_iota(jnp.int32, (size, size), 1)
    ).astype(BF16)
    return jnp.dot(
        jnp.concatenate([first, second, third], axis=1),
        jnp.concatenate([ones, ones, ones], axis=0),
        preferred_element_type=F32,
    )


def chain_kernel(
    peers, x_hbm, z_hbm, b_hbm, c_hbm, step_hbm, gate_hbm, hist_hbm, skip_hbm,
    states, enter, send, coef_ref, fin_ref, y_ref, z_ref, c_ref, grow_ref, start_ref,
    x_ref, b_ref, step_ref, gate_ref, hist_ref, skip_ref, cumul_ref, shift_ref,
    scores_ref, skips_ref, total, their_total, full,
    x_sem, z_sem, c_sem, b_sem, hist_sem, load_sem, send_sem, recv_sem, fin_send_sem, fin_recv_sem,
):
    blocks, heads, size, head_size = x_ref.shape
    count, width = b_ref.shape[1], b_ref.shape[3]
    me = lax.axis_index("seq")
    per_group = heads // count
    share = head_size // peers
    each = -(-heads // blocks)

    def peer(d):
        return dict(device_id={"seq": d}, device_id_type=MESH)

    barrier = pltpu.get_barrier_semaphore()
    for by in range(1, peers):
        pl.semaphore_signal(barrier, inc=1, **peer(lax.rem(me + by, peers)))

    def fetch(source, target, sem, c):
        parts, wide = target.shape[1], target.shape[3]
        for h in range(parts):
            pltpu.make_async_copy(
                source.at[pl.ds(c * size, size), pl.ds(h * wide, wide)],
                target.at[c, h],
                sem.at[c],
            ).start()

    def fetched(target, sem, c):
        pltpu.make_async_copy(target.at[c], target.at[c], sem.at[c]).wait()

    small = [
        pltpu.make_async_copy(gate_hbm, gate_ref, load_sem.at[0]),
        pltpu.make_async_copy(step_hbm, step_ref, load_sem.at[1]),
        pltpu.make_async_copy(skip_hbm, skip_ref, load_sem.at[2]),
    ]
    for copy in small:
        copy.start()

    def hist_copy(c):
        span = pl.ds(jnp.minimum(c * each, heads - each), each)
        return pltpu.make_async_copy(hist_hbm.at[span], hist_ref.at[c], hist_sem.at[c])

    def fetch_first(c, carry):
        fetch(b_hbm, b_ref, b_sem, c)
        fetch(c_hbm, c_ref, c_sem, c)
        fetch(x_hbm, x_ref, x_sem, c)
        hist_copy(c).start()
        return carry

    def fetch_later(c, carry):
        fetch(z_hbm, z_ref, z_sem, c)
        return carry

    lax.fori_loop(0, blocks, fetch_first, 0)
    lax.fori_loop(0, blocks, fetch_later, 0)

    row = lax.broadcasted_iota(jnp.int32, (size, size), 0)
    col = lax.broadcasted_iota(jnp.int32, (size, size), 1)
    eye = (row == col).astype(F32)
    causal = row >= col
    small[2].wait()
    for h in range(heads):
        skips_ref[h] = skip_ref[h] * eye
    small[0].wait()
    small[1].wait()

    rows = [gate_ref[:, c * size : (c + 1) * size] for c in range(blocks)]
    cumul = prefix_sums(jnp.concatenate(rows, axis=0) * LOG2E)
    for c in range(blocks):
        here = cumul[c * heads : (c + 1) * heads]
        cumul_ref[c] = here
        shift_ref[c] = here - jnp.log2(step_ref[:, c * size : (c + 1) * size])

    states[0] = jnp.zeros(states.shape[1:], F32)
    one = jnp.ones((heads, size), F32)

    def arrived(c):
        hist_copy(c).wait()
        fetched(b_ref, b_sem, c)
        fetched(c_ref, c_sem, c)
        fetched(x_ref, x_sem, c)

    def gather_some(i, past):
        for j in range(GATHER):
            arrived(i * GATHER + j)
        for j in range(GATHER):
            past = gather(i * GATHER + j, past)
        return past

    def gather(c, past):
        cumul, shift = cumul_ref[c], shift_ref[c]
        last = jnp.broadcast_to(cumul[:, size - 1 : size], (heads, size))
        decays = jnp.exp2(last)
        tails = jnp.exp2(last - shift)
        start_ref[c] = jnp.exp2(past)
        for g in range(count):
            scores = lax.dot_general(
                c_ref[c, g], b_ref[c, g], (((1,), (1,)), ((), ())), preferred_element_type=F32
            )
            scores_ref[c, g] = jnp.where(causal, scores, 0.0)
            turned = jnp.transpose(b_ref[c, g].astype(F32))
            for k in range(0, per_group, 2):
                pair = range(g * per_group + k, g * per_group + k + 2)
                delta = paired([turned * tails[h : h + 1, :] for h in pair], [x_ref[c, h] for h in pair])
                for j, h in enumerate(pair):
                    states[c + 1, h] = (
                        decays[h : h + 1, :] * states[c, h]
                        + delta[:, j * head_size : (j + 1) * head_size]
                    )
        columns = jnp.transpose(cumul)
        grow_ref[c] = jnp.exp2(columns)
        for h in range(heads):
            y_ref[c, h] = jnp.broadcast_to(columns[:, h : h + 1], (size, size))
        for j in range(each):
            enter[0, jnp.minimum(c * each, heads - each) + j] = jnp.transpose(hist_ref[c, j])
        return past + last

    total[...] = jnp.exp2(lax.fori_loop(0, blocks // GATHER, gather_some, jnp.zeros((heads, size), F32)))
    first = jnp.where(me == 0, total[...], 0.0)

    for h in range(heads):
        send[h] = first[h : h + 1, :] * enter[0, h] + states[blocks, h]
    pl.semaphore_wait(barrier, peers - 1)

    def swap(g):
        span = pl.ds(g * per_group, per_group)
        return pltpu.make_async_remote_copy(
            src_ref=send.at[span], dst_ref=enter.at[1, span],
            send_sem=send_sem.at[g], recv_sem=recv_sem.at[g], **peer(1 - me),
        )

    def swap_total():
        return pltpu.make_async_remote_copy(
            src_ref=total, dst_ref=their_total,
            send_sem=fin_send_sem.at[0, 0], recv_sem=fin_recv_sem.at[0], **peer(1 - me),
        )

    def link(g):
        span = pl.ds(g * per_group, per_group)
        return pltpu.make_async_remote_copy(
            src_ref=send.at[span], dst_ref=enter.at[1, span],
            send_sem=send_sem.at[g], recv_sem=recv_sem.at[g],
            **peer(jnp.minimum(me + 1, peers - 1)),
        )

    def to_peer(d, g):
        span = pl.ds(g * per_group, per_group)
        return pltpu.make_async_remote_copy(
            src_ref=full.at[d, span], dst_ref=fin_ref.at[span],
            send_sem=fin_send_sem.at[d, g], recv_sem=fin_recv_sem.at[g],
            **peer(d),
        )

    if peers == 2:
        for g in range(count):
            swap(g).start()
        swap_total().start()
    else:

        @pl.when(me == 0)
        def _():
            for g in range(count):
                link(g).start()

    def within(c, carry):
        shift = shift_ref[c]
        for g in range(count):
            scores = scores_ref[c, g]
            for k in range(0, per_group, 2):
                pair = range(g * per_group + k, g * per_group + k + 2)
                y = paired(
                    [
                        scores * jnp.exp2(jnp.minimum(y_ref[c, h] - shift[h : h + 1, :], 0.0))
                        + skips_ref[h]
                        for h in pair
                    ],
                    [x_ref[c, h] for h in pair],
                )
                for j, h in enumerate(pair):
                    y_ref[c, h] = y[:, j * head_size : (j + 1) * head_size]
        return carry

    middle = blocks if peers == 2 else (blocks + 1) // 2
    lax.fori_loop(0, middle, within, 0, unroll=WITHIN)

    if peers == 2:
        for g in range(count):
            swap(g).wait()
        swap_total().wait()
        coef_ref[0] = jnp.where(me == 0, their_total[...], one)
        coef_ref[1] = jnp.where(me == 0, one, total[...])
    else:

        @pl.when(me > 0)
        def _():
            for g in range(count):
                link(g).wait_recv()
                for h in range(g * per_group, (g + 1) * per_group):
                    send[h] = total[h : h + 1, :] * enter[1, h] + states[blocks, h]

                @pl.when(me < peers - 1)
                def _(g=g):
                    link(g).start()

                @pl.when(me == peers - 1)
                def _(g=g):
                    for h in range(g * per_group, (g + 1) * per_group):
                        closing = jnp.transpose(send[h])
                        for d in range(peers - 1):
                            full[d, h] = closing[d * share : (d + 1) * share]
                        fin_ref[h] = closing[(peers - 1) * share :]
                    for d in range(peers - 1):
                        to_peer(d, g).start()

        coef_ref[...] = jnp.zeros_like(coef_ref)
        lax.fori_loop(middle, blocks, within, 0)

    def last_fetched(c, carry):
        fetched(z_ref, z_sem, c)
        return carry

    lax.fori_loop(0, blocks, last_fetched, 0)

    if peers == 2:
        fin_ref[...] = jnp.zeros_like(fin_ref)
    else:

        @pl.when(me == peers - 1)
        def _():
            for g in range(count):
                for d in range(peers - 1):
                    to_peer(d, g).wait_send()

        @pl.when(me < peers - 1)
        def _():
            for g in range(count):
                link(g).wait_send()
            for g in range(count):
                to_peer(0, g).wait_recv()


def mix_kernel(
    peers, gain_ref, states, enter, send, coef_ref, fin_ref, y_ref, z_ref, c_ref, grow_ref, start_ref,
    out_hbm, fin_hbm, gated, turned, out_ref, out_sem, fin_sem,
):
    blocks, heads, size, head_size = y_ref.shape
    count, width = c_ref.shape[1], c_ref.shape[3]
    per_group = heads // count
    share = head_size // peers
    each = -(-heads // blocks)

    me = lax.axis_index("seq")
    source = jnp.minimum(me, 1)

    if peers == 2:

        def fin_copy(c):
            span = pl.ds(jnp.minimum(c * each, heads - each), each)
            mine = pl.ds(pl.multiple_of(me * share, share), share)
            return pltpu.make_async_copy(turned.at[c, :, mine], fin_hbm.at[span], fin_sem.at[c])
    else:

        whole_copy = pltpu.make_async_copy(fin_ref, fin_hbm, fin_sem.at[0])
        whole_copy.start()

    def block(c, carry):
        grow, starts = grow_ref[c], start_ref[c]
        if peers == 2:
            for j in range(each):
                h = jnp.minimum(c * each, heads - each) + j
                turned[c, j] = jnp.transpose(
                    coef_ref[0, pl.ds(h, 1), :] * send[h]
                    + coef_ref[1, pl.ds(h, 1), :] * enter[1, h]
                )
        for g in range(count):
            read = c_ref[c, g]
            left = jnp.concatenate([read, read], axis=1)
            squares = jnp.zeros((size, head_size), F32)
            for k in range(0, per_group, 2):
                pair = range(g * per_group + k, g * per_group + k + 2)
                right = [
                    jnp.concatenate(
                        split(states[c, h] + starts[h : h + 1, :] * enter[source, h]), axis=0
                    )
                    for h in pair
                ]
                earlier = jnp.dot(
                    left, jnp.concatenate(right, axis=1), preferred_element_type=F32
                )
                for j, h in enumerate(pair):
                    along = jnp.broadcast_to(grow[:, h : h + 1], (size, head_size))
                    y = y_ref[c, h] + along * earlier[:, j * head_size : (j + 1) * head_size]
                    z = z_ref[c, h].astype(F32)
                    value = y * (z * jax.nn.sigmoid(z))
                    gated[h - g * per_group] = value
                    squares = squares + value * value
            mean = jnp.sum(squares, axis=1, keepdims=True) * (1.0 / (per_group * head_size))
            scale = jnp.broadcast_to(lax.rsqrt(mean + 1e-05), (size, head_size))
            for k in range(per_group):
                h = g * per_group + k
                gain = gain_ref[pl.ds(h * head_size, head_size)].astype(F32).reshape(1, head_size)
                out_ref[c, h] = (gated[k] * scale * gain).astype(BF16)
                pltpu.make_async_copy(
                    out_ref.at[c, h],
                    out_hbm.at[pl.ds(c * size, size), pl.ds(h * head_size, head_size)],
                    out_sem.at[c],
                ).start()
        if peers == 2:
            fin_copy(c).start()
        return carry

    lax.fori_loop(0, blocks, block, 0)

    def sent(c, carry):
        pltpu.make_async_copy(out_ref.at[c], out_ref.at[c], out_sem.at[c]).wait()
        if peers == 2:
            fin_copy(c).wait()
        return carry

    lax.fori_loop(0, blocks, sent, 0)
    if peers > 2:
        whole_copy.wait()


def body(
    values, gate_in, write_proj, read_proj, step_size, log_gate, skip_gain, norm_gain, history
):
    heads, head_size, width = history.shape
    groups = write_proj.shape[1] // width
    rows = values.shape[0]
    peers = lax.axis_size("seq")
    share = head_size // peers
    size = math.gcd(rows, 128)
    blocks = rows // size
    in_vmem = pl.BlockSpec(memory_space=pltpu.VMEM)
    in_hbm = pl.BlockSpec(memory_space=pltpu.HBM)
    dma = pltpu.SemaphoreType.DMA
    relay = heads if peers > 2 else 1
    each = -(-heads // blocks)

    handed = pl.pallas_call(
        functools.partial(chain_kernel, peers),
        in_specs=[in_hbm] * 8,
        out_specs=[in_vmem] * 10,
        out_shape=[
            pltpu.VMEM((blocks + 1, heads, width, head_size), F32),
            pltpu.VMEM((2, heads, width, head_size), F32),
            pltpu.VMEM((heads, width, head_size), F32),
            pltpu.VMEM((2, heads, size), F32),
            pltpu.VMEM((heads if peers > 2 else 1, share, width), F32),
            pltpu.VMEM((blocks, heads, size, head_size), F32),
            pltpu.VMEM((blocks, heads, size, head_size), BF16),
            pltpu.VMEM((blocks, groups, size, width), BF16),
            pltpu.VMEM((blocks, size, heads), F32),
            pltpu.VMEM((blocks, heads, size), F32),
        ],
        scratch_shapes=[
            pltpu.VMEM((blocks, heads, size, head_size), BF16),
            pltpu.VMEM((blocks, groups, size, width), BF16),
            pltpu.VMEM((heads, rows), F32),
            pltpu.VMEM((heads, rows), F32),
            pltpu.VMEM((blocks, each, head_size, width), F32),
            pltpu.SMEM((heads,), F32),
            pltpu.VMEM((blocks, heads, size), F32),
            pltpu.VMEM((blocks, heads, size), F32),
            pltpu.VMEM((blocks, groups, size, size), F32),
            pltpu.VMEM((heads, size, size), F32),
            pltpu.VMEM((heads, size), F32),
            pltpu.VMEM((heads, size), F32),
            pltpu.VMEM((peers - 1, relay, share, width), F32),
            dma((blocks,)),
            dma((blocks,)),
            dma((blocks,)),
            dma((blocks,)),
            dma((blocks,)),
            dma((3,)),
            dma((groups,)),
            dma((groups,)),
            dma((peers - 1, groups)),
            dma((groups,)),
        ],
        compiler_params=pltpu.CompilerParams(
            collective_id=0, has_side_effects=True, vmem_limit_bytes=VMEM
        ),
        name="chain",
    )(
        *(
            pltpu.with_memory_space_constraint(array, pltpu.HBM)
            for array in (
                values, gate_in, write_proj, read_proj, step_size.T, log_gate.T, history,
                skip_gain,
            )
        )
    )

    normed, final_state = pl.pallas_call(
        functools.partial(mix_kernel, peers),
        in_specs=[in_vmem] * 11,
        out_specs=[in_hbm] * 2,
        out_shape=[
            jax.ShapeDtypeStruct((rows, heads * head_size), BF16),
            jax.ShapeDtypeStruct((heads, share, width), F32),
        ],
        scratch_shapes=[
            pltpu.VMEM((heads // groups, size, head_size), F32),
            pltpu.VMEM((blocks, each, head_size, width), F32),
            pltpu.VMEM((blocks, heads, size, head_size), BF16),
            dma((blocks,)),
            dma((blocks,)),
        ],
        compiler_params=pltpu.CompilerParams(vmem_limit_bytes=VMEM),
        name="mix",
    )(norm_gain, *handed)
    return normed, final_state


def solution(mesh):
    rows = P(("batch", "seq"), "tp")
    return jax.shard_map(
        body,
        mesh=mesh,
        in_specs=(rows, rows, rows, rows, rows, rows, P("tp"), P("tp"), P(("batch", "tp"), None, None)),
        out_specs=(rows, P(("batch", "tp"), "seq", None)),
        check_vma=False,
    )
```

```python
import functools
import math

import jax
import jax.numpy as jnp
from jax import lax
from jax.experimental import pallas as pl
from jax.experimental.pallas import tpu as pltpu
from jax.sharding import PartitionSpec as P

VMEM = 20 << 20
LOG2E = math.log2(math.e)
GATHER, WITHIN = 2, 4
MESH = pl.DeviceIdType.MESH
F32 = jnp.float32
BF16 = jnp.bfloat16


def split(value):
    high = value.astype(BF16)
    low = (value - high.astype(F32)).astype(BF16)
    return high, low


def split_wide(value):
    high = value.astype(BF16).astype(F32)
    return jnp.concatenate([high, value - high], axis=1)


def thirds(value):
    first = value.astype(BF16).astype(F32)
    second = (value - first).astype(BF16).astype(F32)
    return first, second, value - first - second


def paired(lefts, rights):
    out = []
    for left, right in zip(lefts, rights):
        high = left.astype(BF16)
        low = (left - high.astype(F32)).astype(BF16)
        out.append(
            jnp.dot(high, right, preferred_element_type=F32)
            + jnp.dot(low, right, preferred_element_type=F32)
        )
    return jnp.concatenate(out, axis=1)


def prefix_sums(rows):
    size = rows.shape[1]
    first, second, third = (part.astype(BF16) for part in thirds(rows))
    ones = (
        lax.broadcasted_iota(jnp.int32, (size, size), 0)
        <= lax.broadcasted_iota(jnp.int32, (size, size), 1)
    ).astype(BF16)
    return jnp.dot(
        jnp.concatenate([first, second, third], axis=1),
        jnp.concatenate([ones, ones, ones], axis=0),
        preferred_element_type=F32,
    )


def chain_kernel(
    peers, x_hbm, z_hbm, b_hbm, c_hbm, step_hbm, gate_hbm, hist_hbm, skip_hbm,
    states, enter, send, coef_ref, fin_ref, y_ref, z_ref, c_ref, grow_ref, start_ref,
    x_ref, b_ref, step_ref, gate_ref, hist_ref, skip_ref, cumul_ref, shift_ref,
    scores_ref, skips_ref, total, their_total, full,
    x_sem, z_sem, c_sem, b_sem, hist_sem, load_sem, send_sem, recv_sem, fin_send_sem, fin_recv_sem,
):
    blocks, heads, size, head_size = x_ref.shape
    count, width = b_ref.shape[1], b_ref.shape[3]
    me = lax.axis_index("seq")
    per_group = heads // count
    share = head_size // peers
    each = -(-heads // blocks)

    def peer(d):
        return dict(device_id={"seq": d}, device_id_type=MESH)

    barrier = pltpu.get_barrier_semaphore()
    for by in range(1, peers):
        pl.semaphore_signal(barrier, inc=1, **peer(lax.rem(me + by, peers)))

    def fetch(source, target, sem, c):
        parts, wide = target.shape[1], target.shape[3]
        for h in range(parts):
            pltpu.make_async_copy(
                source.at[pl.ds(c * size, size), pl.ds(h * wide, wide)],
                target.at[c, h],
                sem.at[c],
            ).start()

    def fetched(target, sem, c):
        pltpu.make_async_copy(target.at[c], target.at[c], sem.at[c]).wait()

    small = [
        pltpu.make_async_copy(gate_hbm, gate_ref, load_sem.at[0]),
        pltpu.make_async_copy(step_hbm, step_ref, load_sem.at[1]),
        pltpu.make_async_copy(skip_hbm, skip_ref, load_sem.at[2]),
    ]
    for copy in small:
        copy.start()

    def hist_copy(c):
        span = pl.ds(jnp.minimum(c * each, heads - each), each)
        return pltpu.make_async_copy(hist_hbm.at[span], hist_ref.at[c], hist_sem.at[c])

    def fetch_first(c, carry):
        fetch(b_hbm, b_ref, b_sem, c)
        fetch(c_hbm, c_ref, c_sem, c)
        fetch(x_hbm, x_ref, x_sem, c)
        hist_copy(c).start()
        return carry

    def fetch_later(c, carry):
        fetch(z_hbm, z_ref, z_sem, c)
        return carry

    lax.fori_loop(0, blocks, fetch_first, 0)
    lax.fori_loop(0, blocks, fetch_later, 0)

    row = lax.broadcasted_iota(jnp.int32, (size, size), 0)
    col = lax.broadcasted_iota(jnp.int32, (size, size), 1)
    eye = (row == col).astype(F32)
    causal = row >= col
    small[2].wait()
    for h in range(heads):
        skips_ref[h] = skip_ref[h] * eye
    small[0].wait()
    small[1].wait()

    rows = [gate_ref[:, c * size : (c + 1) * size] for c in range(blocks)]
    cumul = prefix_sums(jnp.concatenate(rows, axis=0) * LOG2E)
    for c in range(blocks):
        here = cumul[c * heads : (c + 1) * heads]
        cumul_ref[c] = here
        shift_ref[c] = here - jnp.log2(step_ref[:, c * size : (c + 1) * size])

    states[0] = jnp.zeros(states.shape[1:], F32)
    one = jnp.ones((heads, size), F32)

    def arrived(c):
        hist_copy(c).wait()
        fetched(b_ref, b_sem, c)
        fetched(c_ref, c_sem, c)
        fetched(x_ref, x_sem, c)

    def gather_some(i, past):
        for j in range(GATHER):
            arrived(i * GATHER + j)
        for j in range(GATHER):
            past = gather(i * GATHER + j, past)
        return past

    def gather(c, past):
        cumul, shift = cumul_ref[c], shift_ref[c]
        last = jnp.broadcast_to(cumul[:, size - 1 : size], (heads, size))
        decays = jnp.exp2(last)
        tails = jnp.exp2(last - shift)
        start_ref[c] = jnp.exp2(past)
        for g in range(count):
            scores = lax.dot_general(
                c_ref[c, g], b_ref[c, g], (((1,), (1,)), ((), ())), preferred_element_type=F32
            )
            scores_ref[c, g] = jnp.where(causal, scores, 0.0)
            turned = jnp.transpose(b_ref[c, g].astype(F32))
            for k in range(0, per_group, 2):
                pair = range(g * per_group + k, g * per_group + k + 2)
                delta = paired([turned * tails[h : h + 1, :] for h in pair], [x_ref[c, h] for h in pair])
                for j, h in enumerate(pair):
                    states[c + 1, h] = (
                        decays[h : h + 1, :] * states[c, h]
                        + delta[:, j * head_size : (j + 1) * head_size]
                    )
        columns = jnp.transpose(cumul)
        grow_ref[c] = jnp.exp2(columns)
        for h in range(heads):
            y_ref[c, h] = jnp.broadcast_to(columns[:, h : h + 1], (size, size))
        for j in range(each):
            enter[0, jnp.minimum(c * each, heads - each) + j] = jnp.transpose(hist_ref[c, j])
        return past + last

    total[...] = jnp.exp2(lax.fori_loop(0, blocks // GATHER, gather_some, jnp.zeros((heads, size), F32)))
    first = jnp.where(me == 0, total[...], 0.0)

    for h in range(heads):
        send[h] = first[h : h + 1, :] * enter[0, h] + states[blocks, h]
    pl.semaphore_wait(barrier, peers - 1)

    def swap(g):
        span = pl.ds(g * per_group, per_group)
        return pltpu.make_async_remote_copy(
            src_ref=send.at[span], dst_ref=enter.at[1, span],
            send_sem=send_sem.at[g], recv_sem=recv_sem.at[g], **peer(1 - me),
        )

    def swap_total():
        return pltpu.make_async_remote_copy(
            src_ref=total, dst_ref=their_total,
            send_sem=fin_send_sem.at[0, 0], recv_sem=fin_recv_sem.at[0], **peer(1 - me),
        )

    def link(g):
        span = pl.ds(g * per_group, per_group)
        return pltpu.make_async_remote_copy(
            src_ref=send.at[span], dst_ref=enter.at[1, span],
            send_sem=send_sem.at[g], recv_sem=recv_sem.at[g],
            **peer(jnp.minimum(me + 1, peers - 1)),
        )

    def to_peer(d, g):
        span = pl.ds(g * per_group, per_group)
        return pltpu.make_async_remote_copy(
            src_ref=full.at[d, span], dst_ref=fin_ref.at[span],
            send_sem=fin_send_sem.at[d, g], recv_sem=fin_recv_sem.at[g],
            **peer(d),
        )

    if peers == 2:
        for g in range(count):
            swap(g).start()
        swap_total().start()
    else:

        @pl.when(me == 0)
        def _():
            for g in range(count):
                link(g).start()

    def within(c, carry):
        shift = shift_ref[c]
        for g in range(count):
            scores = scores_ref[c, g]
            for k in range(0, per_group, 2):
                pair = range(g * per_group + k, g * per_group + k + 2)
                y = paired(
                    [
                        scores * jnp.exp2(jnp.minimum(y_ref[c, h] - shift[h : h + 1, :], 0.0))
                        + skips_ref[h]
                        for h in pair
                    ],
                    [x_ref[c, h] for h in pair],
                )
                for j, h in enumerate(pair):
                    y_ref[c, h] = y[:, j * head_size : (j + 1) * head_size]
        return carry

    middle = blocks if peers == 2 else (blocks + 1) // 2
    lax.fori_loop(0, middle, within, 0, unroll=WITHIN)

    if peers == 2:
        for g in range(count):
            swap(g).wait()
        swap_total().wait()
        coef_ref[0] = jnp.where(me == 0, their_total[...], one)
        coef_ref[1] = jnp.where(me == 0, one, total[...])
    else:

        @pl.when(me > 0)
        def _():
            for g in range(count):
                link(g).wait_recv()
                for h in range(g * per_group, (g + 1) * per_group):
                    send[h] = total[h : h + 1, :] * enter[1, h] + states[blocks, h]

                @pl.when(me < peers - 1)
                def _(g=g):
                    link(g).start()

                @pl.when(me == peers - 1)
                def _(g=g):
                    for h in range(g * per_group, (g + 1) * per_group):
                        closing = jnp.transpose(send[h])
                        for d in range(peers - 1):
                            full[d, h] = closing[d * share : (d + 1) * share]
                        fin_ref[h] = closing[(peers - 1) * share :]
                    for d in range(peers - 1):
                        to_peer(d, g).start()

        coef_ref[...] = jnp.zeros_like(coef_ref)
        lax.fori_loop(middle, blocks, within, 0)

    def last_fetched(c, carry):
        fetched(z_ref, z_sem, c)
        return carry

    lax.fori_loop(0, blocks, last_fetched, 0)

    if peers == 2:
        fin_ref[...] = jnp.zeros_like(fin_ref)
    else:

        @pl.when(me == peers - 1)
        def _():
            for g in range(count):
                for d in range(peers - 1):
                    to_peer(d, g).wait_send()

        @pl.when(me < peers - 1)
        def _():
            for g in range(count):
                link(g).wait_send()
            for g in range(count):
                to_peer(0, g).wait_recv()


def mix_kernel(
    peers, gain_ref, states, enter, send, coef_ref, fin_ref, y_ref, z_ref, c_ref, grow_ref, start_ref,
    out_hbm, fin_hbm, gated, turned, out_ref, out_sem, fin_sem,
):
    blocks, heads, size, head_size = y_ref.shape
    count, width = c_ref.shape[1], c_ref.shape[3]
    per_group = heads // count
    share = head_size // peers
    each = -(-heads // blocks)

    me = lax.axis_index("seq")
    source = jnp.minimum(me, 1)

    if peers == 2:

        def fin_copy(c):
            span = pl.ds(jnp.minimum(c * each, heads - each), each)
            mine = pl.ds(pl.multiple_of(me * share, share), share)
            return pltpu.make_async_copy(turned.at[c, :, mine], fin_hbm.at[span], fin_sem.at[c])
    else:

        whole_copy = pltpu.make_async_copy(fin_ref, fin_hbm, fin_sem.at[0])
        whole_copy.start()

    def block(c, carry):
        grow, starts = grow_ref[c], start_ref[c]
        if peers == 2:
            for j in range(each):
                h = jnp.minimum(c * each, heads - each) + j
                turned[c, j] = jnp.transpose(
                    coef_ref[0, pl.ds(h, 1), :] * send[h]
                    + coef_ref[1, pl.ds(h, 1), :] * enter[1, h]
                )
        for g in range(count):
            read = c_ref[c, g]
            left = jnp.concatenate([read, read], axis=1)
            squares = jnp.zeros((size, head_size), F32)
            for k in range(0, per_group, 2):
                pair = range(g * per_group + k, g * per_group + k + 2)
                right = [
                    jnp.concatenate(
                        split(states[c, h] + starts[h : h + 1, :] * enter[source, h]), axis=0
                    )
                    for h in pair
                ]
                earlier = jnp.dot(
                    left, jnp.concatenate(right, axis=1), preferred_element_type=F32
                )
                for j, h in enumerate(pair):
                    along = jnp.broadcast_to(grow[:, h : h + 1], (size, head_size))
                    y = y_ref[c, h] + along * earlier[:, j * head_size : (j + 1) * head_size]
                    z = z_ref[c, h].astype(F32)
                    value = y * (z * jax.nn.sigmoid(z))
                    gated[h - g * per_group] = value
                    squares = squares + value * value
            mean = jnp.sum(squares, axis=1, keepdims=True) * (1.0 / (per_group * head_size))
            scale = jnp.broadcast_to(lax.rsqrt(mean + 1e-05), (size, head_size))
            for k in range(per_group):
                h = g * per_group + k
                gain = gain_ref[pl.ds(h * head_size, head_size)].astype(F32).reshape(1, head_size)
                out_ref[c, h] = (gated[k] * scale * gain).astype(BF16)
                pltpu.make_async_copy(
                    out_ref.at[c, h],
                    out_hbm.at[pl.ds(c * size, size), pl.ds(h * head_size, head_size)],
                    out_sem.at[c],
                ).start()
        if peers == 2:
            fin_copy(c).start()
        return carry

    lax.fori_loop(0, blocks, block, 0)

    def sent(c, carry):
        pltpu.make_async_copy(out_ref.at[c], out_ref.at[c], out_sem.at[c]).wait()
        if peers == 2:
            fin_copy(c).wait()
        return carry

    lax.fori_loop(0, blocks, sent, 0)
    if peers > 2:
        whole_copy.wait()


def body(
    values, gate_in, write_proj, read_proj, step_size, log_gate, skip_gain, norm_gain, history
):
    heads, head_size, width = history.shape
    groups = write_proj.shape[1] // width
    rows = values.shape[0]
    peers = lax.axis_size("seq")
    share = head_size // peers
    size = math.gcd(rows, 128)
    blocks = rows // size
    in_vmem = pl.BlockSpec(memory_space=pltpu.VMEM)
    in_hbm = pl.BlockSpec(memory_space=pltpu.HBM)
    dma = pltpu.SemaphoreType.DMA
    relay = heads if peers > 2 else 1
    each = -(-heads // blocks)

    handed = pl.pallas_call(
        functools.partial(chain_kernel, peers),
        in_specs=[in_hbm] * 8,
        out_specs=[in_vmem] * 10,
        out_shape=[
            pltpu.VMEM((blocks + 1, heads, width, head_size), F32),
            pltpu.VMEM((2, heads, width, head_size), F32),
            pltpu.VMEM((heads, width, head_size), F32),
            pltpu.VMEM((2, heads, size), F32),
            pltpu.VMEM((heads if peers > 2 else 1, share, width), F32),
            pltpu.VMEM((blocks, heads, size, head_size), F32),
            pltpu.VMEM((blocks, heads, size, head_size), BF16),
            pltpu.VMEM((blocks, groups, size, width), BF16),
            pltpu.VMEM((blocks, size, heads), F32),
            pltpu.VMEM((blocks, heads, size), F32),
        ],
        scratch_shapes=[
            pltpu.VMEM((blocks, heads, size, head_size), BF16),
            pltpu.VMEM((blocks, groups, size, width), BF16),
            pltpu.VMEM((heads, rows), F32),
            pltpu.VMEM((heads, rows), F32),
            pltpu.VMEM((blocks, each, head_size, width), F32),
            pltpu.SMEM((heads,), F32),
            pltpu.VMEM((blocks, heads, size), F32),
            pltpu.VMEM((blocks, heads, size), F32),
            pltpu.VMEM((blocks, groups, size, size), F32),
            pltpu.VMEM((heads, size, size), F32),
            pltpu.VMEM((heads, size), F32),
            pltpu.VMEM((heads, size), F32),
            pltpu.VMEM((peers - 1, relay, share, width), F32),
            dma((blocks,)),
            dma((blocks,)),
            dma((blocks,)),
            dma((blocks,)),
            dma((blocks,)),
            dma((3,)),
            dma((groups,)),
            dma((groups,)),
            dma((peers - 1, groups)),
            dma((groups,)),
        ],
        compiler_params=pltpu.CompilerParams(
            collective_id=0, has_side_effects=True, vmem_limit_bytes=VMEM
        ),
        name="chain",
    )(
        *(
            pltpu.with_memory_space_constraint(array, pltpu.HBM)
            for array in (
                values, gate_in, write_proj, read_proj, step_size.T, log_gate.T, history,
                skip_gain,
            )
        )
    )

    normed, final_state = pl.pallas_call(
        functools.partial(mix_kernel, peers),
        in_specs=[in_vmem] * 11,
        out_specs=[in_hbm] * 2,
        out_shape=[
            jax.ShapeDtypeStruct((rows, heads * head_size), BF16),
            jax.ShapeDtypeStruct((heads, share, width), F32),
        ],
        scratch_shapes=[
            pltpu.VMEM((heads // groups, size, head_size), F32),
            pltpu.VMEM((blocks, each, head_size, width), F32),
            pltpu.VMEM((blocks, heads, size, head_size), BF16),
            dma((blocks,)),
            dma((blocks,)),
        ],
        compiler_params=pltpu.CompilerParams(vmem_limit_bytes=VMEM),
        name="mix",
    )(norm_gain, *handed)
    return normed, final_state


def solution(mesh):
    rows = P(("batch", "seq"), "tp")
    return jax.shard_map(
        body,
        mesh=mesh,
        in_specs=(rows, rows, rows, rows, rows, rows, P("tp"), P("tp"), P(("batch", "tp"), None, None)),
        out_specs=(rows, P(("batch", "tp"), "seq", None)),
        check_vma=False,
    )
```

```python
import functools
import math

import jax
import jax.numpy as jnp
from jax import lax
from jax.experimental import pallas as pl
from jax.experimental.pallas import tpu as pltpu
from jax.sharding import PartitionSpec as P

VMEM = 20 << 20
LOG2E = math.log2(math.e)
GATHER, WITHIN = 2, 4
MESH = pl.DeviceIdType.MESH
F32 = jnp.float32
BF16 = jnp.bfloat16


def split(value):
    high = value.astype(BF16)
    low = (value - high.astype(F32)).astype(BF16)
    return high, low


def split_wide(value):
    high = value.astype(BF16).astype(F32)
    return jnp.concatenate([high, value - high], axis=1)


def thirds(value):
    first = value.astype(BF16).astype(F32)
    second = (value - first).astype(BF16).astype(F32)
    return first, second, value - first - second


def paired(lefts, rights):
    out = []
    for left, right in zip(lefts, rights):
        high = left.astype(BF16)
        low = (left - high.astype(F32)).astype(BF16)
        out.append(
            jnp.dot(high, right, preferred_element_type=F32)
            + jnp.dot(low, right, preferred_element_type=F32)
        )
    return jnp.concatenate(out, axis=1)


def prefix_sums(rows):
    size = rows.shape[1]
    first, second, third = (part.astype(BF16) for part in thirds(rows))
    ones = (
        lax.broadcasted_iota(jnp.int32, (size, size), 0)
        <= lax.broadcasted_iota(jnp.int32, (size, size), 1)
    ).astype(BF16)
    return jnp.dot(
        jnp.concatenate([first, second, third], axis=1),
        jnp.concatenate([ones, ones, ones], axis=0),
        preferred_element_type=F32,
    )


def chain_kernel(
    peers, x_hbm, z_hbm, b_hbm, c_hbm, step_hbm, gate_hbm, hist_hbm, skip_hbm,
    states, enter, send, coef_ref, fin_ref, y_ref, z_ref, c_ref, grow_ref, start_ref,
    x_ref, b_ref, step_ref, gate_ref, hist_ref, skip_ref, cumul_ref, shift_ref,
    scores_ref, skips_ref, total, their_total, full,
    x_sem, z_sem, c_sem, b_sem, hist_sem, load_sem, send_sem, recv_sem, fin_send_sem, fin_recv_sem,
):
    blocks, heads, size, head_size = x_ref.shape
    count, width = b_ref.shape[1], b_ref.shape[3]
    me = lax.axis_index("seq")
    per_group = heads // count
    share = head_size // peers
    each = -(-heads // blocks)

    def peer(d):
        return dict(device_id={"seq": d}, device_id_type=MESH)

    barrier = pltpu.get_barrier_semaphore()
    for by in range(1, peers):
        pl.semaphore_signal(barrier, inc=1, **peer(lax.rem(me + by, peers)))

    def fetch(source, target, sem, c):
        parts, wide = target.shape[1], target.shape[3]
        for h in range(parts):
            pltpu.make_async_copy(
                source.at[pl.ds(c * size, size), pl.ds(h * wide, wide)],
                target.at[c, h],
                sem.at[c],
            ).start()

    def fetched(target, sem, c):
        pltpu.make_async_copy(target.at[c], target.at[c], sem.at[c]).wait()

    small = [
        pltpu.make_async_copy(gate_hbm, gate_ref, load_sem.at[0]),
        pltpu.make_async_copy(step_hbm, step_ref, load_sem.at[1]),
        pltpu.make_async_copy(skip_hbm, skip_ref, load_sem.at[2]),
    ]
    for copy in small:
        copy.start()

    def hist_copy(c):
        span = pl.ds(jnp.minimum(c * each, heads - each), each)
        return pltpu.make_async_copy(hist_hbm.at[span], hist_ref.at[c], hist_sem.at[c])

    def fetch_first(c, carry):
        fetch(b_hbm, b_ref, b_sem, c)
        fetch(c_hbm, c_ref, c_sem, c)
        fetch(x_hbm, x_ref, x_sem, c)
        hist_copy(c).start()
        return carry

    def fetch_later(c, carry):
        fetch(z_hbm, z_ref, z_sem, c)
        return carry

    lax.fori_loop(0, blocks, fetch_first, 0)
    lax.fori_loop(0, blocks, fetch_later, 0)

    row = lax.broadcasted_iota(jnp.int32, (size, size), 0)
    col = lax.broadcasted_iota(jnp.int32, (size, size), 1)
    eye = (row == col).astype(F32)
    causal = row >= col
    small[2].wait()
    for h in range(heads):
        skips_ref[h] = skip_ref[h] * eye
    small[0].wait()
    small[1].wait()

    rows = [gate_ref[:, c * size : (c + 1) * size] for c in range(blocks)]
    cumul = prefix_sums(jnp.concatenate(rows, axis=0) * LOG2E)
    for c in range(blocks):
        here = cumul[c * heads : (c + 1) * heads]
        cumul_ref[c] = here
        shift_ref[c] = here - jnp.log2(step_ref[:, c * size : (c + 1) * size])

    states[0] = jnp.zeros(states.shape[1:], F32)
    one = jnp.ones((heads, size), F32)

    def arrived(c):
        hist_copy(c).wait()
        fetched(b_ref, b_sem, c)
        fetched(c_ref, c_sem, c)
        fetched(x_ref, x_sem, c)

    def gather_some(i, past):
        for j in range(GATHER):
            arrived(i * GATHER + j)
        for j in range(GATHER):
            past = gather(i * GATHER + j, past)
        return past

    def gather(c, past):
        cumul, shift = cumul_ref[c], shift_ref[c]
        last = jnp.broadcast_to(cumul[:, size - 1 : size], (heads, size))
        decays = jnp.exp2(last)
        tails = jnp.exp2(last - shift)
        start_ref[c] = jnp.exp2(past)
        for g in range(count):
            scores = lax.dot_general(
                c_ref[c, g], b_ref[c, g], (((1,), (1,)), ((), ())), preferred_element_type=F32
            )
            scores_ref[c, g] = jnp.where(causal, scores, 0.0)
            turned = jnp.transpose(b_ref[c, g].astype(F32))
            for k in range(0, per_group, 2):
                pair = range(g * per_group + k, g * per_group + k + 2)
                delta = paired([turned * tails[h : h + 1, :] for h in pair], [x_ref[c, h] for h in pair])
                for j, h in enumerate(pair):
                    states[c + 1, h] = (
                        decays[h : h + 1, :] * states[c, h]
                        + delta[:, j * head_size : (j + 1) * head_size]
                    )
        columns = jnp.transpose(cumul)
        grow_ref[c] = jnp.exp2(columns)
        for h in range(heads):
            y_ref[c, h] = jnp.broadcast_to(columns[:, h : h + 1], (size, size))
        for j in range(each):
            enter[0, jnp.minimum(c * each, heads - each) + j] = jnp.transpose(hist_ref[c, j])
        return past + last

    total[...] = jnp.exp2(lax.fori_loop(0, blocks // GATHER, gather_some, jnp.zeros((heads, size), F32)))
    first = jnp.where(me == 0, total[...], 0.0)

    for h in range(heads):
        send[h] = first[h : h + 1, :] * enter[0, h] + states[blocks, h]
    pl.semaphore_wait(barrier, peers - 1)

    def swap(g):
        span = pl.ds(g * per_group, per_group)
        return pltpu.make_async_remote_copy(
            src_ref=send.at[span], dst_ref=enter.at[1, span],
            send_sem=send_sem.at[g], recv_sem=recv_sem.at[g], **peer(1 - me),
        )

    def swap_total():
        return pltpu.make_async_remote_copy(
            src_ref=total, dst_ref=their_total,
            send_sem=fin_send_sem.at[0, 0], recv_sem=fin_recv_sem.at[0], **peer(1 - me),
        )

    def link(g):
        span = pl.ds(g * per_group, per_group)
        return pltpu.make_async_remote_copy(
            src_ref=send.at[span], dst_ref=enter.at[1, span],
            send_sem=send_sem.at[g], recv_sem=recv_sem.at[g],
            **peer(jnp.minimum(me + 1, peers - 1)),
        )

    def to_peer(d, g):
        span = pl.ds(g * per_group, per_group)
        return pltpu.make_async_remote_copy(
            src_ref=full.at[d, span], dst_ref=fin_ref.at[span],
            send_sem=fin_send_sem.at[d, g], recv_sem=fin_recv_sem.at[g],
            **peer(d),
        )

    if peers == 2:
        for g in range(count):
            swap(g).start()
        swap_total().start()
    else:

        @pl.when(me == 0)
        def _():
            for g in range(count):
                link(g).start()

    def within(c, carry):
        shift = shift_ref[c]
        for g in range(count):
            scores = scores_ref[c, g]
            for k in range(0, per_group, 2):
                pair = range(g * per_group + k, g * per_group + k + 2)
                y = paired(
                    [
                        scores * jnp.exp2(jnp.minimum(y_ref[c, h] - shift[h : h + 1, :], 0.0))
                        + skips_ref[h]
                        for h in pair
                    ],
                    [x_ref[c, h] for h in pair],
                )
                for j, h in enumerate(pair):
                    y_ref[c, h] = y[:, j * head_size : (j + 1) * head_size]
        return carry

    middle = blocks if peers == 2 else (blocks + 1) // 2
    lax.fori_loop(0, middle, within, 0, unroll=WITHIN)

    if peers == 2:
        for g in range(count):
            swap(g).wait()
        swap_total().wait()
        coef_ref[0] = jnp.where(me == 0, their_total[...], one)
        coef_ref[1] = jnp.where(me == 0, one, total[...])
    else:

        @pl.when(me > 0)
        def _():
            for g in range(count):
                link(g).wait_recv()
                for h in range(g * per_group, (g + 1) * per_group):
                    send[h] = total[h : h + 1, :] * enter[1, h] + states[blocks, h]

                @pl.when(me < peers - 1)
                def _(g=g):
                    link(g).start()

                @pl.when(me == peers - 1)
                def _(g=g):
                    for h in range(g * per_group, (g + 1) * per_group):
                        closing = jnp.transpose(send[h])
                        for d in range(peers - 1):
                            full[d, h] = closing[d * share : (d + 1) * share]
                        fin_ref[h] = closing[(peers - 1) * share :]
                    for d in range(peers - 1):
                        to_peer(d, g).start()

        coef_ref[...] = jnp.zeros_like(coef_ref)
        lax.fori_loop(middle, blocks, within, 0)

    def last_fetched(c, carry):
        fetched(z_ref, z_sem, c)
        return carry

    lax.fori_loop(0, blocks, last_fetched, 0)

    if peers == 2:
        fin_ref[...] = jnp.zeros_like(fin_ref)
    else:

        @pl.when(me == peers - 1)
        def _():
            for g in range(count):
                for d in range(peers - 1):
                    to_peer(d, g).wait_send()

        @pl.when(me < peers - 1)
        def _():
            for g in range(count):
                link(g).wait_send()
            for g in range(count):
                to_peer(0, g).wait_recv()


def mix_kernel(
    peers, gain_ref, states, enter, send, coef_ref, fin_ref, y_ref, z_ref, c_ref, grow_ref, start_ref,
    out_hbm, fin_hbm, gated, turned, out_ref, out_sem, fin_sem,
):
    blocks, heads, size, head_size = y_ref.shape
    count, width = c_ref.shape[1], c_ref.shape[3]
    per_group = heads // count
    share = head_size // peers
    each = -(-heads // blocks)

    me = lax.axis_index("seq")
    source = jnp.minimum(me, 1)

    if peers == 2:

        def fin_copy(c):
            span = pl.ds(jnp.minimum(c * each, heads - each), each)
            mine = pl.ds(pl.multiple_of(me * share, share), share)
            return pltpu.make_async_copy(turned.at[c, :, mine], fin_hbm.at[span], fin_sem.at[c])
    else:

        whole_copy = pltpu.make_async_copy(fin_ref, fin_hbm, fin_sem.at[0])
        whole_copy.start()

    eye = (
        lax.broadcasted_iota(jnp.int32, (head_size, head_size), 0)
        == lax.broadcasted_iota(jnp.int32, (head_size, head_size), 1)
    ).astype(F32).astype(BF16)

    def block(c, carry):
        grow, starts = grow_ref[c], start_ref[c]
        if peers == 2:
            for j in range(each):
                h = jnp.minimum(c * each, heads - each) + j
                turned[c, j] = jnp.transpose(
                    coef_ref[0, pl.ds(h, 1), :] * send[h]
                    + coef_ref[1, pl.ds(h, 1), :] * enter[1, h]
                )
        for g in range(count):
            read = c_ref[c, g]
            left = jnp.concatenate([read, read], axis=1)
            squares = jnp.zeros((size, head_size), F32)
            for k in range(0, per_group, 2):
                pair = range(g * per_group + k, g * per_group + k + 2)
                right = [
                    jnp.concatenate(
                        split(states[c, h] + starts[h : h + 1, :] * enter[source, h]), axis=0
                    )
                    for h in pair
                ]
                earlier = jnp.dot(
                    left, jnp.concatenate(right, axis=1), preferred_element_type=F32
                )
                for j, h in enumerate(pair):
                    along = jnp.broadcast_to(grow[:, h : h + 1], (size, head_size))
                    y = y_ref[c, h] + along * earlier[:, j * head_size : (j + 1) * head_size]
                    z = jnp.dot(z_ref[c, h], eye, preferred_element_type=F32)
                    value = y * (z * jax.nn.sigmoid(z))
                    gated[h - g * per_group] = value
                    squares = squares + value * value
            mean = jnp.sum(squares, axis=1, keepdims=True) * (1.0 / (per_group * head_size))
            scale = jnp.broadcast_to(lax.rsqrt(mean + 1e-05), (size, head_size))
            for k in range(per_group):
                h = g * per_group + k
                gain = gain_ref[pl.ds(h * head_size, head_size)].astype(F32).reshape(1, head_size)
                out_ref[c, h] = (gated[k] * scale * gain).astype(BF16)
                pltpu.make_async_copy(
                    out_ref.at[c, h],
                    out_hbm.at[pl.ds(c * size, size), pl.ds(h * head_size, head_size)],
                    out_sem.at[c],
                ).start()
        if peers == 2:
            fin_copy(c).start()
        return carry

    lax.fori_loop(0, blocks, block, 0, unroll=2)

    def sent(c, carry):
        pltpu.make_async_copy(out_ref.at[c], out_ref.at[c], out_sem.at[c]).wait()
        if peers == 2:
            fin_copy(c).wait()
        return carry

    lax.fori_loop(0, blocks, sent, 0)
    if peers > 2:
        whole_copy.wait()


def body(
    values, gate_in, write_proj, read_proj, step_size, log_gate, skip_gain, norm_gain, history
):
    heads, head_size, width = history.shape
    groups = write_proj.shape[1] // width
    rows = values.shape[0]
    peers = lax.axis_size("seq")
    share = head_size // peers
    size = math.gcd(rows, 128)
    blocks = rows // size
    in_vmem = pl.BlockSpec(memory_space=pltpu.VMEM)
    in_hbm = pl.BlockSpec(memory_space=pltpu.HBM)
    dma = pltpu.SemaphoreType.DMA
    relay = heads if peers > 2 else 1
    each = -(-heads // blocks)

    handed = pl.pallas_call(
        functools.partial(chain_kernel, peers),
        in_specs=[in_hbm] * 8,
        out_specs=[in_vmem] * 10,
        out_shape=[
            pltpu.VMEM((blocks + 1, heads, width, head_size), F32),
            pltpu.VMEM((2, heads, width, head_size), F32),
            pltpu.VMEM((heads, width, head_size), F32),
            pltpu.VMEM((2, heads, size), F32),
            pltpu.VMEM((heads if peers > 2 else 1, share, width), F32),
            pltpu.VMEM((blocks, heads, size, head_size), F32),
            pltpu.VMEM((blocks, heads, size, head_size), BF16),
            pltpu.VMEM((blocks, groups, size, width), BF16),
            pltpu.VMEM((blocks, size, heads), F32),
            pltpu.VMEM((blocks, heads, size), F32),
        ],
        scratch_shapes=[
            pltpu.VMEM((blocks, heads, size, head_size), BF16),
            pltpu.VMEM((blocks, groups, size, width), BF16),
            pltpu.VMEM((heads, rows), F32),
            pltpu.VMEM((heads, rows), F32),
            pltpu.VMEM((blocks, each, head_size, width), F32),
            pltpu.SMEM((heads,), F32),
            pltpu.VMEM((blocks, heads, size), F32),
            pltpu.VMEM((blocks, heads, size), F32),
            pltpu.VMEM((blocks, groups, size, size), F32),
            pltpu.VMEM((heads, size, size), F32),
            pltpu.VMEM((heads, size), F32),
            pltpu.VMEM((heads, size), F32),
            pltpu.VMEM((peers - 1, relay, share, width), F32),
            dma((blocks,)),
            dma((blocks,)),
            dma((blocks,)),
            dma((blocks,)),
            dma((blocks,)),
            dma((3,)),
            dma((groups,)),
            dma((groups,)),
            dma((peers - 1, groups)),
            dma((groups,)),
        ],
        compiler_params=pltpu.CompilerParams(
            collective_id=0, has_side_effects=True, vmem_limit_bytes=VMEM
        ),
        name="chain",
    )(
        *(
            pltpu.with_memory_space_constraint(array, pltpu.HBM)
            for array in (
                values, gate_in, write_proj, read_proj, step_size.T, log_gate.T, history,
                skip_gain,
            )
        )
    )

    normed, final_state = pl.pallas_call(
        functools.partial(mix_kernel, peers),
        in_specs=[in_vmem] * 11,
        out_specs=[in_hbm] * 2,
        out_shape=[
            jax.ShapeDtypeStruct((rows, heads * head_size), BF16),
            jax.ShapeDtypeStruct((heads, share, width), F32),
        ],
        scratch_shapes=[
            pltpu.VMEM((heads // groups, size, head_size), F32),
            pltpu.VMEM((blocks, each, head_size, width), F32),
            pltpu.VMEM((blocks, heads, size, head_size), BF16),
            dma((blocks,)),
            dma((blocks,)),
        ],
        compiler_params=pltpu.CompilerParams(vmem_limit_bytes=VMEM),
        name="mix",
    )(norm_gain, *handed)
    return normed, final_state


def solution(mesh):
    rows = P(("batch", "seq"), "tp")
    return jax.shard_map(
        body,
        mesh=mesh,
        in_specs=(rows, rows, rows, rows, rows, rows, P("tp"), P("tp"), P(("batch", "tp"), None, None)),
        out_specs=(rows, P(("batch", "tp"), "seq", None)),
        check_vma=False,
    )
```

```python
import functools
import math

import jax
import jax.numpy as jnp
from jax import lax
from jax.experimental import pallas as pl
from jax.experimental.pallas import tpu as pltpu
from jax.sharding import PartitionSpec as P

VMEM = 20 << 20
LOG2E = math.log2(math.e)
GATHER, WITHIN = 2, 4
MESH = pl.DeviceIdType.MESH
F32 = jnp.float32
BF16 = jnp.bfloat16


def split(value):
    high = value.astype(BF16)
    low = (value - high.astype(F32)).astype(BF16)
    return high, low


def split_wide(value):
    high = value.astype(BF16).astype(F32)
    return jnp.concatenate([high, value - high], axis=1)


def thirds(value):
    first = value.astype(BF16).astype(F32)
    second = (value - first).astype(BF16).astype(F32)
    return first, second, value - first - second


def paired(lefts, rights):
    out = []
    for left, right in zip(lefts, rights):
        high = left.astype(BF16)
        low = (left - high.astype(F32)).astype(BF16)
        out.append(
            jnp.dot(high, right, preferred_element_type=F32)
            + jnp.dot(low, right, preferred_element_type=F32)
        )
    return jnp.concatenate(out, axis=1)


def prefix_sums(rows):
    size = rows.shape[1]
    first, second, third = (part.astype(BF16) for part in thirds(rows))
    ones = (
        lax.broadcasted_iota(jnp.int32, (size, size), 0)
        <= lax.broadcasted_iota(jnp.int32, (size, size), 1)
    ).astype(BF16)
    return jnp.dot(
        jnp.concatenate([first, second, third], axis=1),
        jnp.concatenate([ones, ones, ones], axis=0),
        preferred_element_type=F32,
    )


def chain_kernel(
    peers, x_hbm, z_hbm, b_hbm, c_hbm, step_hbm, gate_hbm, hist_hbm, skip_hbm,
    states, enter, send, coef_ref, fin_ref, y_ref, z_ref, c_ref, grow_ref, start_ref,
    x_ref, b_ref, step_ref, gate_ref, hist_ref, skip_ref, cumul_ref, shift_ref,
    scores_ref, skips_ref, total, their_total, full,
    x_sem, z_sem, c_sem, b_sem, hist_sem, load_sem, send_sem, recv_sem, fin_send_sem, fin_recv_sem,
):
    blocks, heads, size, head_size = x_ref.shape
    count, width = b_ref.shape[1], b_ref.shape[3]
    me = lax.axis_index("seq")
    per_group = heads // count
    share = head_size // peers
    each = -(-heads // blocks)

    def peer(d):
        return dict(device_id={"seq": d}, device_id_type=MESH)

    barrier = pltpu.get_barrier_semaphore()
    for by in range(1, peers):
        pl.semaphore_signal(barrier, inc=1, **peer(lax.rem(me + by, peers)))

    def fetch(source, target, sem, c):
        parts, wide = target.shape[1], target.shape[3]
        for h in range(parts):
            pltpu.make_async_copy(
                source.at[pl.ds(c * size, size), pl.ds(h * wide, wide)],
                target.at[c, h],
                sem.at[c],
            ).start()

    def fetched(target, sem, c):
        pltpu.make_async_copy(target.at[c], target.at[c], sem.at[c]).wait()

    small = [
        pltpu.make_async_copy(gate_hbm, gate_ref, load_sem.at[0]),
        pltpu.make_async_copy(step_hbm, step_ref, load_sem.at[1]),
        pltpu.make_async_copy(skip_hbm, skip_ref, load_sem.at[2]),
    ]
    for copy in small:
        copy.start()

    def hist_copy(c):
        span = pl.ds(jnp.minimum(c * each, heads - each), each)
        return pltpu.make_async_copy(hist_hbm.at[span], hist_ref.at[c], hist_sem.at[c])

    def fetch_first(c, carry):
        fetch(b_hbm, b_ref, b_sem, c)
        fetch(c_hbm, c_ref, c_sem, c)
        fetch(x_hbm, x_ref, x_sem, c)
        hist_copy(c).start()
        return carry

    def fetch_later(c, carry):
        fetch(z_hbm, z_ref, z_sem, c)
        return carry

    lax.fori_loop(0, blocks, fetch_first, 0)
    lax.fori_loop(0, blocks, fetch_later, 0)

    row = lax.broadcasted_iota(jnp.int32, (size, size), 0)
    col = lax.broadcasted_iota(jnp.int32, (size, size), 1)
    eye = (row == col).astype(F32)
    causal = row >= col
    small[2].wait()
    for h in range(heads):
        skips_ref[h] = skip_ref[h] * eye
    small[0].wait()
    small[1].wait()

    rows = [gate_ref[:, c * size : (c + 1) * size] for c in range(blocks)]
    cumul = prefix_sums(jnp.concatenate(rows, axis=0) * LOG2E)
    for c in range(blocks):
        here = cumul[c * heads : (c + 1) * heads]
        cumul_ref[c] = here
        shift_ref[c] = here - jnp.log2(step_ref[:, c * size : (c + 1) * size])

    states[0] = jnp.zeros(states.shape[1:], F32)
    one = jnp.ones((heads, size), F32)

    def arrived(c):
        hist_copy(c).wait()
        fetched(b_ref, b_sem, c)
        fetched(c_ref, c_sem, c)
        fetched(x_ref, x_sem, c)

    def gather_some(i, past):
        for j in range(GATHER):
            arrived(i * GATHER + j)
        for j in range(GATHER):
            past = gather(i * GATHER + j, past)
        return past

    def gather(c, past):
        cumul, shift = cumul_ref[c], shift_ref[c]
        last = jnp.broadcast_to(cumul[:, size - 1 : size], (heads, size))
        decays = jnp.exp2(last)
        tails = jnp.exp2(last - shift)
        start_ref[c] = jnp.exp2(past)
        for g in range(count):
            scores = lax.dot_general(
                c_ref[c, g], b_ref[c, g], (((1,), (1,)), ((), ())), preferred_element_type=F32
            )
            scores_ref[c, g] = jnp.where(causal, scores, 0.0)
            turned = jnp.transpose(b_ref[c, g].astype(F32))
            for k in range(0, per_group, 2):
                pair = range(g * per_group + k, g * per_group + k + 2)
                delta = paired([turned * tails[h : h + 1, :] for h in pair], [x_ref[c, h] for h in pair])
                for j, h in enumerate(pair):
                    states[c + 1, h] = (
                        decays[h : h + 1, :] * states[c, h]
                        + delta[:, j * head_size : (j + 1) * head_size]
                    )
        columns = jnp.transpose(cumul)
        for h in range(heads):
            along = jnp.broadcast_to(columns[:, h : h + 1], (size, size))
            y_ref[c, h] = along
            grow_ref[c, h] = jnp.exp2(along)
        for j in range(each):
            enter[0, jnp.minimum(c * each, heads - each) + j] = jnp.transpose(hist_ref[c, j])
        return past + last

    total[...] = jnp.exp2(lax.fori_loop(0, blocks // GATHER, gather_some, jnp.zeros((heads, size), F32)))
    first = jnp.where(me == 0, total[...], 0.0)

    for h in range(heads):
        send[h] = first[h : h + 1, :] * enter[0, h] + states[blocks, h]
    pl.semaphore_wait(barrier, peers - 1)

    def swap(g):
        span = pl.ds(g * per_group, per_group)
        return pltpu.make_async_remote_copy(
            src_ref=send.at[span], dst_ref=enter.at[1, span],
            send_sem=send_sem.at[g], recv_sem=recv_sem.at[g], **peer(1 - me),
        )

    def swap_total():
        return pltpu.make_async_remote_copy(
            src_ref=total, dst_ref=their_total,
            send_sem=fin_send_sem.at[0, 0], recv_sem=fin_recv_sem.at[0], **peer(1 - me),
        )

    def link(g):
        span = pl.ds(g * per_group, per_group)
        return pltpu.make_async_remote_copy(
            src_ref=send.at[span], dst_ref=enter.at[1, span],
            send_sem=send_sem.at[g], recv_sem=recv_sem.at[g],
            **peer(jnp.minimum(me + 1, peers - 1)),
        )

    def to_peer(d, g):
        span = pl.ds(g * per_group, per_group)
        return pltpu.make_async_remote_copy(
            src_ref=full.at[d, span], dst_ref=fin_ref.at[span],
            send_sem=fin_send_sem.at[d, g], recv_sem=fin_recv_sem.at[g],
            **peer(d),
        )

    if peers == 2:
        for g in range(count):
            swap(g).start()
        swap_total().start()
    else:

        @pl.when(me == 0)
        def _():
            for g in range(count):
                link(g).start()

    def within(c, carry):
        shift = shift_ref[c]
        for g in range(count):
            scores = scores_ref[c, g]
            for k in range(0, per_group, 2):
                pair = range(g * per_group + k, g * per_group + k + 2)
                y = paired(
                    [
                        scores * jnp.exp2(jnp.minimum(y_ref[c, h] - shift[h : h + 1, :], 0.0))
                        + skips_ref[h]
                        for h in pair
                    ],
                    [x_ref[c, h] for h in pair],
                )
                for j, h in enumerate(pair):
                    y_ref[c, h] = y[:, j * head_size : (j + 1) * head_size]
        return carry

    middle = blocks if peers == 2 else (blocks + 1) // 2
    lax.fori_loop(0, middle, within, 0, unroll=WITHIN)

    if peers == 2:
        for g in range(count):
            swap(g).wait()
        swap_total().wait()
        coef_ref[0] = jnp.where(me == 0, their_total[...], one)
        coef_ref[1] = jnp.where(me == 0, one, total[...])
    else:

        @pl.when(me > 0)
        def _():
            for g in range(count):
                link(g).wait_recv()
                for h in range(g * per_group, (g + 1) * per_group):
                    send[h] = total[h : h + 1, :] * enter[1, h] + states[blocks, h]

                @pl.when(me < peers - 1)
                def _(g=g):
                    link(g).start()

                @pl.when(me == peers - 1)
                def _(g=g):
                    for h in range(g * per_group, (g + 1) * per_group):
                        closing = jnp.transpose(send[h])
                        for d in range(peers - 1):
                            full[d, h] = closing[d * share : (d + 1) * share]
                        fin_ref[h] = closing[(peers - 1) * share :]
                    for d in range(peers - 1):
                        to_peer(d, g).start()

        coef_ref[...] = jnp.zeros_like(coef_ref)
        lax.fori_loop(middle, blocks, within, 0)

    def last_fetched(c, carry):
        fetched(z_ref, z_sem, c)
        return carry

    lax.fori_loop(0, blocks, last_fetched, 0)

    if peers == 2:
        fin_ref[...] = jnp.zeros_like(fin_ref)
    else:

        @pl.when(me == peers - 1)
        def _():
            for g in range(count):
                for d in range(peers - 1):
                    to_peer(d, g).wait_send()

        @pl.when(me < peers - 1)
        def _():
            for g in range(count):
                link(g).wait_send()
            for g in range(count):
                to_peer(0, g).wait_recv()


def mix_kernel(
    peers, gain_ref, states, enter, send, coef_ref, fin_ref, y_ref, z_ref, c_ref, grow_ref, start_ref,
    out_hbm, fin_hbm, gated, turned, out_ref, out_sem, fin_sem,
):
    blocks, heads, size, head_size = y_ref.shape
    count, width = c_ref.shape[1], c_ref.shape[3]
    per_group = heads // count
    share = head_size // peers
    each = -(-heads // blocks)

    me = lax.axis_index("seq")
    source = jnp.minimum(me, 1)

    if peers == 2:

        def fin_copy(c):
            span = pl.ds(jnp.minimum(c * each, heads - each), each)
            mine = pl.ds(pl.multiple_of(me * share, share), share)
            return pltpu.make_async_copy(turned.at[c, :, mine], fin_hbm.at[span], fin_sem.at[c])
    else:

        whole_copy = pltpu.make_async_copy(fin_ref, fin_hbm, fin_sem.at[0])
        whole_copy.start()

    eye = (
        lax.broadcasted_iota(jnp.int32, (head_size, head_size), 0)
        == lax.broadcasted_iota(jnp.int32, (head_size, head_size), 1)
    ).astype(F32).astype(BF16)

    def block(c, carry):
        starts = start_ref[c]
        if peers == 2:
            for j in range(each):
                h = jnp.minimum(c * each, heads - each) + j
                turned[c, j] = jnp.transpose(
                    coef_ref[0, pl.ds(h, 1), :] * send[h]
                    + coef_ref[1, pl.ds(h, 1), :] * enter[1, h]
                )
        for g in range(count):
            read = c_ref[c, g]
            left = jnp.concatenate([read, read], axis=1)
            squares = jnp.zeros((size, head_size), F32)
            for k in range(0, per_group, 2):
                pair = range(g * per_group + k, g * per_group + k + 2)
                right = [
                    jnp.concatenate(
                        split(states[c, h] + starts[h : h + 1, :] * enter[source, h]), axis=0
                    )
                    for h in pair
                ]
                earlier = jnp.dot(
                    left, jnp.concatenate(right, axis=1), preferred_element_type=F32
                )
                for j, h in enumerate(pair):
                    along = grow_ref[c, h]
                    y = y_ref[c, h] + along * earlier[:, j * head_size : (j + 1) * head_size]
                    z = jnp.dot(z_ref[c, h], eye, preferred_element_type=F32)
                    value = y * (z * jax.nn.sigmoid(z))
                    gated[h - g * per_group] = value
                    squares = squares + value * value
            mean = jnp.sum(squares, axis=1, keepdims=True) * (1.0 / (per_group * head_size))
            scale = jnp.broadcast_to(lax.rsqrt(mean + 1e-05), (size, head_size))
            for k in range(per_group):
                h = g * per_group + k
                gain = gain_ref[pl.ds(h * head_size, head_size)].astype(F32).reshape(1, head_size)
                out_ref[c, h] = (gated[k] * scale * gain).astype(BF16)
                pltpu.make_async_copy(
                    out_ref.at[c, h],
                    out_hbm.at[pl.ds(c * size, size), pl.ds(h * head_size, head_size)],
                    out_sem.at[c],
                ).start()
        if peers == 2:
            fin_copy(c).start()
        return carry

    lax.fori_loop(0, blocks, block, 0, unroll=2)

    def sent(c, carry):
        pltpu.make_async_copy(out_ref.at[c], out_ref.at[c], out_sem.at[c]).wait()
        if peers == 2:
            fin_copy(c).wait()
        return carry

    lax.fori_loop(0, blocks, sent, 0)
    if peers > 2:
        whole_copy.wait()


def body(
    values, gate_in, write_proj, read_proj, step_size, log_gate, skip_gain, norm_gain, history
):
    heads, head_size, width = history.shape
    groups = write_proj.shape[1] // width
    rows = values.shape[0]
    peers = lax.axis_size("seq")
    share = head_size // peers
    size = math.gcd(rows, 128)
    blocks = rows // size
    in_vmem = pl.BlockSpec(memory_space=pltpu.VMEM)
    in_hbm = pl.BlockSpec(memory_space=pltpu.HBM)
    dma = pltpu.SemaphoreType.DMA
    relay = heads if peers > 2 else 1
    each = -(-heads // blocks)

    handed = pl.pallas_call(
        functools.partial(chain_kernel, peers),
        in_specs=[in_hbm] * 8,
        out_specs=[in_vmem] * 10,
        out_shape=[
            pltpu.VMEM((blocks + 1, heads, width, head_size), F32),
            pltpu.VMEM((2, heads, width, head_size), F32),
            pltpu.VMEM((heads, width, head_size), F32),
            pltpu.VMEM((2, heads, size), F32),
            pltpu.VMEM((heads if peers > 2 else 1, share, width), F32),
            pltpu.VMEM((blocks, heads, size, head_size), F32),
            pltpu.VMEM((blocks, heads, size, head_size), BF16),
            pltpu.VMEM((blocks, groups, size, width), BF16),
            pltpu.VMEM((blocks, heads, size, head_size), F32),
            pltpu.VMEM((blocks, heads, size), F32),
        ],
        scratch_shapes=[
            pltpu.VMEM((blocks, heads, size, head_size), BF16),
            pltpu.VMEM((blocks, groups, size, width), BF16),
            pltpu.VMEM((heads, rows), F32),
            pltpu.VMEM((heads, rows), F32),
            pltpu.VMEM((blocks, each, head_size, width), F32),
            pltpu.SMEM((heads,), F32),
            pltpu.VMEM((blocks, heads, size), F32),
            pltpu.VMEM((blocks, heads, size), F32),
            pltpu.VMEM((blocks, groups, size, size), F32),
            pltpu.VMEM((heads, size, size), F32),
            pltpu.VMEM((heads, size), F32),
            pltpu.VMEM((heads, size), F32),
            pltpu.VMEM((peers - 1, relay, share, width), F32),
            dma((blocks,)),
            dma((blocks,)),
            dma((blocks,)),
            dma((blocks,)),
            dma((blocks,)),
            dma((3,)),
            dma((groups,)),
            dma((groups,)),
            dma((peers - 1, groups)),
            dma((groups,)),
        ],
        compiler_params=pltpu.CompilerParams(
            collective_id=0, has_side_effects=True, vmem_limit_bytes=VMEM
        ),
        name="chain",
    )(
        *(
            pltpu.with_memory_space_constraint(array, pltpu.HBM)
            for array in (
                values, gate_in, write_proj, read_proj, step_size.T, log_gate.T, history,
                skip_gain,
            )
        )
    )

    normed, final_state = pl.pallas_call(
        functools.partial(mix_kernel, peers),
        in_specs=[in_vmem] * 11,
        out_specs=[in_hbm] * 2,
        out_shape=[
            jax.ShapeDtypeStruct((rows, heads * head_size), BF16),
            jax.ShapeDtypeStruct((heads, share, width), F32),
        ],
        scratch_shapes=[
            pltpu.VMEM((heads // groups, size, head_size), F32),
            pltpu.VMEM((blocks, each, head_size, width), F32),
            pltpu.VMEM((blocks, heads, size, head_size), BF16),
            dma((blocks,)),
            dma((blocks,)),
        ],
        compiler_params=pltpu.CompilerParams(vmem_limit_bytes=VMEM),
        name="mix",
    )(norm_gain, *handed)
    return normed, final_state


def solution(mesh):
    rows = P(("batch", "seq"), "tp")
    return jax.shard_map(
        body,
        mesh=mesh,
        in_specs=(rows, rows, rows, rows, rows, rows, P("tp"), P("tp"), P(("batch", "tp"), None, None)),
        out_specs=(rows, P(("batch", "tp"), "seq", None)),
        check_vma=False,
    )
```

```python
import functools
import math

import jax
import jax.numpy as jnp
from jax import lax
from jax.experimental import pallas as pl
from jax.experimental.pallas import tpu as pltpu
from jax.sharding import PartitionSpec as P

VMEM = 20 << 20
LOG2E = math.log2(math.e)
GATHER, WITHIN = 2, 4
MESH = pl.DeviceIdType.MESH
F32 = jnp.float32
BF16 = jnp.bfloat16


def split(value):
    high = value.astype(BF16)
    low = (value - high.astype(F32)).astype(BF16)
    return high, low


def split_wide(value):
    high = value.astype(BF16).astype(F32)
    return jnp.concatenate([high, value - high], axis=1)


def thirds(value):
    first = value.astype(BF16).astype(F32)
    second = (value - first).astype(BF16).astype(F32)
    return first, second, value - first - second


def paired(lefts, rights):
    out = []
    for left, right in zip(lefts, rights):
        high = left.astype(BF16)
        low = (left - high.astype(F32)).astype(BF16)
        out.append(
            jnp.dot(high, right, preferred_element_type=F32)
            + jnp.dot(low, right, preferred_element_type=F32)
        )
    return jnp.concatenate(out, axis=1)


def prefix_sums(rows):
    size = rows.shape[1]
    first, second, third = (part.astype(BF16) for part in thirds(rows))
    ones = (
        lax.broadcasted_iota(jnp.int32, (size, size), 0)
        <= lax.broadcasted_iota(jnp.int32, (size, size), 1)
    ).astype(BF16)
    return jnp.dot(
        jnp.concatenate([first, second, third], axis=1),
        jnp.concatenate([ones, ones, ones], axis=0),
        preferred_element_type=F32,
    )


def chain_kernel(
    peers, x_hbm, z_hbm, b_hbm, c_hbm, step_hbm, gate_hbm, hist_hbm, skip_hbm,
    states, enter, send, coef_ref, fin_ref, y_ref, z_ref, c_ref, grow_ref, start_ref,
    x_ref, b_ref, step_ref, gate_ref, hist_ref, skip_ref, cumul_ref, shift_ref,
    scores_ref, skips_ref, total, their_total, full,
    x_sem, z_sem, c_sem, b_sem, hist_sem, load_sem, send_sem, recv_sem, fin_send_sem, fin_recv_sem,
):
    blocks, heads, size, head_size = x_ref.shape
    count, width = b_ref.shape[1], b_ref.shape[3]
    me = lax.axis_index("seq")
    per_group = heads // count
    share = head_size // peers
    each = -(-heads // blocks)

    def peer(d):
        return dict(device_id={"seq": d}, device_id_type=MESH)

    barrier = pltpu.get_barrier_semaphore()
    for by in range(1, peers):
        pl.semaphore_signal(barrier, inc=1, **peer(lax.rem(me + by, peers)))

    def fetch(source, target, sem, c):
        parts, wide = target.shape[1], target.shape[3]
        for h in range(parts):
            pltpu.make_async_copy(
                source.at[pl.ds(c * size, size), pl.ds(h * wide, wide)],
                target.at[c, h],
                sem.at[c],
            ).start()

    def fetched(target, sem, c):
        pltpu.make_async_copy(target.at[c], target.at[c], sem.at[c]).wait()

    small = [
        pltpu.make_async_copy(gate_hbm, gate_ref, load_sem.at[0]),
        pltpu.make_async_copy(step_hbm, step_ref, load_sem.at[1]),
        pltpu.make_async_copy(skip_hbm, skip_ref, load_sem.at[2]),
    ]
    for copy in small:
        copy.start()

    def hist_copy(c):
        span = pl.ds(jnp.minimum(c * each, heads - each), each)
        return pltpu.make_async_copy(hist_hbm.at[span], hist_ref.at[c], hist_sem.at[c])

    def fetch_first(c, carry):
        fetch(b_hbm, b_ref, b_sem, c)
        fetch(c_hbm, c_ref, c_sem, c)
        fetch(x_hbm, x_ref, x_sem, c)
        hist_copy(c).start()
        return carry

    def fetch_later(c, carry):
        fetch(z_hbm, z_ref, z_sem, c)
        return carry

    lax.fori_loop(0, blocks, fetch_first, 0)
    lax.fori_loop(0, blocks, fetch_later, 0)

    row = lax.broadcasted_iota(jnp.int32, (size, size), 0)
    col = lax.broadcasted_iota(jnp.int32, (size, size), 1)
    eye = (row == col).astype(F32)
    causal = row >= col
    states[0] = jnp.zeros(states.shape[1:], F32)
    small[2].wait()
    for h in range(heads):
        skips_ref[h] = skip_ref[h] * eye
    small[0].wait()
    small[1].wait()

    rows = [gate_ref[:, c * size : (c + 1) * size] for c in range(blocks)]
    cumul = prefix_sums(jnp.concatenate(rows, axis=0) * LOG2E)
    for c in range(blocks):
        here = cumul[c * heads : (c + 1) * heads]
        cumul_ref[c] = here
        shift_ref[c] = here - jnp.log2(step_ref[:, c * size : (c + 1) * size])

    one = jnp.ones((heads, size), F32)

    def arrived(c):
        hist_copy(c).wait()
        fetched(b_ref, b_sem, c)
        fetched(c_ref, c_sem, c)
        fetched(x_ref, x_sem, c)

    def gather_some(i, past):
        for j in range(GATHER):
            arrived(i * GATHER + j)
        for j in range(GATHER):
            past = gather(i * GATHER + j, past)
        return past

    def gather(c, past):
        cumul, shift = cumul_ref[c], shift_ref[c]
        last = jnp.broadcast_to(cumul[:, size - 1 : size], (heads, size))
        decays = jnp.exp2(last)
        tails = jnp.exp2(last - shift)
        start_ref[c] = jnp.exp2(past)
        for g in range(count):
            scores = lax.dot_general(
                c_ref[c, g], b_ref[c, g], (((1,), (1,)), ((), ())), preferred_element_type=F32
            )
            scores_ref[c, g] = jnp.where(causal, scores, 0.0)
            turned = jnp.transpose(b_ref[c, g].astype(F32))
            for k in range(0, per_group, 2):
                pair = range(g * per_group + k, g * per_group + k + 2)
                delta = paired([turned * tails[h : h + 1, :] for h in pair], [x_ref[c, h] for h in pair])
                for j, h in enumerate(pair):
                    states[c + 1, h] = (
                        decays[h : h + 1, :] * states[c, h]
                        + delta[:, j * head_size : (j + 1) * head_size]
                    )
        columns = jnp.transpose(cumul)
        for h in range(heads):
            along = jnp.broadcast_to(columns[:, h : h + 1], (size, size))
            y_ref[c, h] = along
            grow_ref[c, h] = jnp.exp2(along)
        for j in range(each):
            enter[0, jnp.minimum(c * each, heads - each) + j] = jnp.transpose(hist_ref[c, j])
        return past + last

    total[...] = jnp.exp2(lax.fori_loop(0, blocks // GATHER, gather_some, jnp.zeros((heads, size), F32)))
    first = jnp.where(me == 0, total[...], 0.0)

    for h in range(heads):
        send[h] = first[h : h + 1, :] * enter[0, h] + states[blocks, h]
    pl.semaphore_wait(barrier, peers - 1)

    def swap(g):
        span = pl.ds(g * per_group, per_group)
        return pltpu.make_async_remote_copy(
            src_ref=send.at[span], dst_ref=enter.at[1, span],
            send_sem=send_sem.at[g], recv_sem=recv_sem.at[g], **peer(1 - me),
        )

    def swap_total():
        return pltpu.make_async_remote_copy(
            src_ref=total, dst_ref=their_total,
            send_sem=fin_send_sem.at[0, 0], recv_sem=fin_recv_sem.at[0], **peer(1 - me),
        )

    def link(g):
        span = pl.ds(g * per_group, per_group)
        return pltpu.make_async_remote_copy(
            src_ref=send.at[span], dst_ref=enter.at[1, span],
            send_sem=send_sem.at[g], recv_sem=recv_sem.at[g],
            **peer(jnp.minimum(me + 1, peers - 1)),
        )

    def to_peer(d, g):
        span = pl.ds(g * per_group, per_group)
        return pltpu.make_async_remote_copy(
            src_ref=full.at[d, span], dst_ref=fin_ref.at[span],
            send_sem=fin_send_sem.at[d, g], recv_sem=fin_recv_sem.at[g],
            **peer(d),
        )

    if peers == 2:
        for g in range(count):
            swap(g).start()
        swap_total().start()
    else:

        @pl.when(me == 0)
        def _():
            for g in range(count):
                link(g).start()

    def within(c, carry):
        shift = shift_ref[c]
        for g in range(count):
            scores = scores_ref[c, g]
            for k in range(0, per_group, 2):
                pair = range(g * per_group + k, g * per_group + k + 2)
                y = paired(
                    [
                        scores * jnp.exp2(jnp.minimum(y_ref[c, h] - shift[h : h + 1, :], 0.0))
                        + skips_ref[h]
                        for h in pair
                    ],
                    [x_ref[c, h] for h in pair],
                )
                for j, h in enumerate(pair):
                    y_ref[c, h] = y[:, j * head_size : (j + 1) * head_size]
        return carry

    middle = blocks if peers == 2 else (blocks + 1) // 2
    lax.fori_loop(0, middle, within, 0, unroll=WITHIN)

    if peers == 2:
        for g in range(count):
            swap(g).wait()
        swap_total().wait()
        coef_ref[0] = jnp.where(me == 0, their_total[...], one)
        coef_ref[1] = jnp.where(me == 0, one, total[...])
    else:

        @pl.when(me > 0)
        def _():
            for g in range(count):
                link(g).wait_recv()
                for h in range(g * per_group, (g + 1) * per_group):
                    send[h] = total[h : h + 1, :] * enter[1, h] + states[blocks, h]

                @pl.when(me < peers - 1)
                def _(g=g):
                    link(g).start()

                @pl.when(me == peers - 1)
                def _(g=g):
                    for h in range(g * per_group, (g + 1) * per_group):
                        closing = jnp.transpose(send[h])
                        for d in range(peers - 1):
                            full[d, h] = closing[d * share : (d + 1) * share]
                        fin_ref[h] = closing[(peers - 1) * share :]
                    for d in range(peers - 1):
                        to_peer(d, g).start()

        coef_ref[...] = jnp.zeros_like(coef_ref)
        lax.fori_loop(middle, blocks, within, 0)

    def last_fetched(c, carry):
        fetched(z_ref, z_sem, c)
        return carry

    lax.fori_loop(0, blocks, last_fetched, 0)

    if peers == 2:
        fin_ref[...] = jnp.zeros_like(fin_ref)
    else:

        @pl.when(me == peers - 1)
        def _():
            for g in range(count):
                for d in range(peers - 1):
                    to_peer(d, g).wait_send()

        @pl.when(me < peers - 1)
        def _():
            for g in range(count):
                link(g).wait_send()
            for g in range(count):
                to_peer(0, g).wait_recv()


def mix_kernel(
    peers, gain_ref, states, enter, send, coef_ref, fin_ref, y_ref, z_ref, c_ref, grow_ref, start_ref,
    out_hbm, fin_hbm, gated, turned, out_ref, out_sem, fin_sem,
):
    blocks, heads, size, head_size = y_ref.shape
    count, width = c_ref.shape[1], c_ref.shape[3]
    per_group = heads // count
    share = head_size // peers
    each = -(-heads // blocks)

    me = lax.axis_index("seq")
    source = jnp.minimum(me, 1)

    if peers == 2:

        def fin_copy(c):
            span = pl.ds(jnp.minimum(c * each, heads - each), each)
            mine = pl.ds(pl.multiple_of(me * share, share), share)
            return pltpu.make_async_copy(turned.at[c, :, mine], fin_hbm.at[span], fin_sem.at[c])
    else:

        whole_copy = pltpu.make_async_copy(fin_ref, fin_hbm, fin_sem.at[0])
        whole_copy.start()

    eye = (
        lax.broadcasted_iota(jnp.int32, (head_size, head_size), 0)
        == lax.broadcasted_iota(jnp.int32, (head_size, head_size), 1)
    ).astype(F32).astype(BF16)

    def block(c, carry):
        starts = start_ref[c]
        if peers == 2:
            for j in range(each):
                h = jnp.minimum(c * each, heads - each) + j
                turned[c, j] = jnp.transpose(
                    coef_ref[0, pl.ds(h, 1), :] * send[h]
                    + coef_ref[1, pl.ds(h, 1), :] * enter[1, h]
                )
        for g in range(count):
            read = c_ref[c, g]
            left = jnp.concatenate([read, read], axis=1)
            squares = jnp.zeros((size, head_size), F32)
            for k in range(0, per_group, 2):
                pair = range(g * per_group + k, g * per_group + k + 2)
                right = [
                    jnp.concatenate(
                        split(states[c, h] + starts[h : h + 1, :] * enter[source, h]), axis=0
                    )
                    for h in pair
                ]
                earlier = jnp.dot(
                    left, jnp.concatenate(right, axis=1), preferred_element_type=F32
                )
                for j, h in enumerate(pair):
                    along = grow_ref[c, h]
                    y = y_ref[c, h] + along * earlier[:, j * head_size : (j + 1) * head_size]
                    z = z_ref[c, h].astype(F32)
                    if j == 0:
                        z = jnp.dot(z_ref[c, h], eye, preferred_element_type=F32)
                    value = y * (z * jax.nn.sigmoid(z))
                    gated[h - g * per_group] = value
                    squares = squares + value * value
            mean = jnp.sum(squares, axis=1, keepdims=True) * (1.0 / (per_group * head_size))
            scale = jnp.broadcast_to(lax.rsqrt(mean + 1e-05), (size, head_size))
            for k in range(per_group):
                h = g * per_group + k
                gain = gain_ref[pl.ds(h * head_size, head_size)].astype(F32).reshape(1, head_size)
                out_ref[c, h] = (gated[k] * scale * gain).astype(BF16)
                pltpu.make_async_copy(
                    out_ref.at[c, h],
                    out_hbm.at[pl.ds(c * size, size), pl.ds(h * head_size, head_size)],
                    out_sem.at[c],
                ).start()
        if peers == 2:
            fin_copy(c).start()
        return carry

    lax.fori_loop(0, blocks, block, 0, unroll=2)

    def sent(c, carry):
        pltpu.make_async_copy(out_ref.at[c], out_ref.at[c], out_sem.at[c]).wait()
        if peers == 2:
            fin_copy(c).wait()
        return carry

    lax.fori_loop(0, blocks, sent, 0)
    if peers > 2:
        whole_copy.wait()


def body(
    values, gate_in, write_proj, read_proj, step_size, log_gate, skip_gain, norm_gain, history
):
    heads, head_size, width = history.shape
    groups = write_proj.shape[1] // width
    rows = values.shape[0]
    peers = lax.axis_size("seq")
    share = head_size // peers
    size = math.gcd(rows, 128)
    blocks = rows // size
    in_vmem = pl.BlockSpec(memory_space=pltpu.VMEM)
    in_hbm = pl.BlockSpec(memory_space=pltpu.HBM)
    dma = pltpu.SemaphoreType.DMA
    relay = heads if peers > 2 else 1
    each = -(-heads // blocks)

    handed = pl.pallas_call(
        functools.partial(chain_kernel, peers),
        in_specs=[in_hbm] * 8,
        out_specs=[in_vmem] * 10,
        out_shape=[
            pltpu.VMEM((blocks + 1, heads, width, head_size), F32),
            pltpu.VMEM((2, heads, width, head_size), F32),
            pltpu.VMEM((heads, width, head_size), F32),
            pltpu.VMEM((2, heads, size), F32),
            pltpu.VMEM((heads if peers > 2 else 1, share, width), F32),
            pltpu.VMEM((blocks, heads, size, head_size), F32),
            pltpu.VMEM((blocks, heads, size, head_size), BF16),
            pltpu.VMEM((blocks, groups, size, width), BF16),
            pltpu.VMEM((blocks, heads, size, head_size), F32),
            pltpu.VMEM((blocks, heads, size), F32),
        ],
        scratch_shapes=[
            pltpu.VMEM((blocks, heads, size, head_size), BF16),
            pltpu.VMEM((blocks, groups, size, width), BF16),
            pltpu.VMEM((heads, rows), F32),
            pltpu.VMEM((heads, rows), F32),
            pltpu.VMEM((blocks, each, head_size, width), F32),
            pltpu.SMEM((heads,), F32),
            pltpu.VMEM((blocks, heads, size), F32),
            pltpu.VMEM((blocks, heads, size), F32),
            pltpu.VMEM((blocks, groups, size, size), F32),
            pltpu.VMEM((heads, size, size), F32),
            pltpu.VMEM((heads, size), F32),
            pltpu.VMEM((heads, size), F32),
            pltpu.VMEM((peers - 1, relay, share, width), F32),
            dma((blocks,)),
            dma((blocks,)),
            dma((blocks,)),
            dma((blocks,)),
            dma((blocks,)),
            dma((3,)),
            dma((groups,)),
            dma((groups,)),
            dma((peers - 1, groups)),
            dma((groups,)),
        ],
        compiler_params=pltpu.CompilerParams(
            collective_id=0, has_side_effects=True, vmem_limit_bytes=VMEM
        ),
        name="chain",
    )(
        *(
            pltpu.with_memory_space_constraint(array, pltpu.HBM)
            for array in (
                values, gate_in, write_proj, read_proj, step_size.T, log_gate.T, history,
                skip_gain,
            )
        )
    )

    normed, final_state = pl.pallas_call(
        functools.partial(mix_kernel, peers),
        in_specs=[in_vmem] * 11,
        out_specs=[in_hbm] * 2,
        out_shape=[
            jax.ShapeDtypeStruct((rows, heads * head_size), BF16),
            jax.ShapeDtypeStruct((heads, share, width), F32),
        ],
        scratch_shapes=[
            pltpu.VMEM((heads // groups, size, head_size), F32),
            pltpu.VMEM((blocks, each, head_size, width), F32),
            pltpu.VMEM((blocks, heads, size, head_size), BF16),
            dma((blocks,)),
            dma((blocks,)),
        ],
        compiler_params=pltpu.CompilerParams(vmem_limit_bytes=VMEM),
        name="mix",
    )(norm_gain, *handed)
    return normed, final_state


def solution(mesh):
    rows = P(("batch", "seq"), "tp")
    return jax.shard_map(
        body,
        mesh=mesh,
        in_specs=(rows, rows, rows, rows, rows, rows, P("tp"), P("tp"), P(("batch", "tp"), None, None)),
        out_specs=(rows, P(("batch", "tp"), "seq", None)),
        check_vma=False,
    )
```

```python
import functools
import math

import jax
import jax.numpy as jnp
from jax import lax
from jax.experimental import pallas as pl
from jax.experimental.pallas import tpu as pltpu
from jax.sharding import PartitionSpec as P

VMEM = 20 << 20
LOG2E = math.log2(math.e)
GATHER, WITHIN = 2, 8
MESH = pl.DeviceIdType.MESH
F32 = jnp.float32
BF16 = jnp.bfloat16


def split(value):
    high = value.astype(BF16)
    low = (value - high.astype(F32)).astype(BF16)
    return high, low


def split_wide(value):
    high = value.astype(BF16).astype(F32)
    return jnp.concatenate([high, value - high], axis=1)


def thirds(value):
    first = value.astype(BF16).astype(F32)
    second = (value - first).astype(BF16).astype(F32)
    return first, second, value - first - second


def paired(lefts, rights):
    out = []
    for left, right in zip(lefts, rights):
        high = left.astype(BF16)
        low = (left - high.astype(F32)).astype(BF16)
        out.append(
            jnp.dot(high, right, preferred_element_type=F32)
            + jnp.dot(low, right, preferred_element_type=F32)
        )
    return jnp.concatenate(out, axis=1)


def prefix_sums(rows):
    size = rows.shape[1]
    first, second, third = (part.astype(BF16) for part in thirds(rows))
    ones = (
        lax.broadcasted_iota(jnp.int32, (size, size), 0)
        <= lax.broadcasted_iota(jnp.int32, (size, size), 1)
    ).astype(BF16)
    return jnp.dot(
        jnp.concatenate([first, second, third], axis=1),
        jnp.concatenate([ones, ones, ones], axis=0),
        preferred_element_type=F32,
    )


def chain_kernel(
    peers, x_hbm, z_hbm, b_hbm, c_hbm, step_hbm, gate_hbm, hist_hbm, skip_hbm,
    states, enter, send, coef_ref, fin_ref, y_ref, z_ref, c_ref, grow_ref, start_ref,
    x_ref, b_ref, step_ref, gate_ref, hist_ref, skip_ref, cumul_ref, shift_ref,
    scores_ref, skips_ref, total, their_total, full,
    x_sem, z_sem, c_sem, b_sem, hist_sem, load_sem, send_sem, recv_sem, fin_send_sem, fin_recv_sem,
):
    blocks, heads, size, head_size = x_ref.shape
    count, width = b_ref.shape[1], b_ref.shape[3]
    me = lax.axis_index("seq")
    per_group = heads // count
    share = head_size // peers
    each = -(-heads // blocks)

    def peer(d):
        return dict(device_id={"seq": d}, device_id_type=MESH)

    barrier = pltpu.get_barrier_semaphore()
    for by in range(1, peers):
        pl.semaphore_signal(barrier, inc=1, **peer(lax.rem(me + by, peers)))

    def fetch(source, target, sem, c):
        parts, wide = target.shape[1], target.shape[3]
        for h in range(parts):
            pltpu.make_async_copy(
                source.at[pl.ds(c * size, size), pl.ds(h * wide, wide)],
                target.at[c, h],
                sem.at[c],
            ).start()

    def fetched(target, sem, c):
        pltpu.make_async_copy(target.at[c], target.at[c], sem.at[c]).wait()

    small = [
        pltpu.make_async_copy(gate_hbm, gate_ref, load_sem.at[0]),
        pltpu.make_async_copy(step_hbm, step_ref, load_sem.at[1]),
        pltpu.make_async_copy(skip_hbm, skip_ref, load_sem.at[2]),
    ]
    for copy in small:
        copy.start()

    def hist_copy(c):
        span = pl.ds(jnp.minimum(c * each, heads - each), each)
        return pltpu.make_async_copy(hist_hbm.at[span], hist_ref.at[c], hist_sem.at[c])

    def fetch_first(c, carry):
        fetch(b_hbm, b_ref, b_sem, c)
        fetch(c_hbm, c_ref, c_sem, c)
        fetch(x_hbm, x_ref, x_sem, c)
        hist_copy(c).start()
        return carry

    def fetch_later(c, carry):
        fetch(z_hbm, z_ref, z_sem, c)
        return carry

    lax.fori_loop(0, blocks, fetch_first, 0)
    lax.fori_loop(0, blocks, fetch_later, 0)

    row = lax.broadcasted_iota(jnp.int32, (size, size), 0)
    col = lax.broadcasted_iota(jnp.int32, (size, size), 1)
    eye = (row == col).astype(F32)
    causal = row >= col
    states[0] = jnp.zeros(states.shape[1:], F32)
    small[2].wait()
    for h in range(heads):
        skips_ref[h] = skip_ref[h] * eye
    small[0].wait()
    small[1].wait()

    rows = [gate_ref[:, c * size : (c + 1) * size] for c in range(blocks)]
    cumul = prefix_sums(jnp.concatenate(rows, axis=0) * LOG2E)
    for c in range(blocks):
        here = cumul[c * heads : (c + 1) * heads]
        cumul_ref[c] = here
        shift_ref[c] = here - jnp.log2(step_ref[:, c * size : (c + 1) * size])

    one = jnp.ones((heads, size), F32)

    def arrived(c):
        hist_copy(c).wait()
        fetched(b_ref, b_sem, c)
        fetched(c_ref, c_sem, c)
        fetched(x_ref, x_sem, c)

    def gather_some(i, past):
        for j in range(GATHER):
            arrived(i * GATHER + j)
        for j in range(GATHER):
            past = gather(i * GATHER + j, past)
        return past

    def gather(c, past):
        cumul, shift = cumul_ref[c], shift_ref[c]
        last = jnp.broadcast_to(cumul[:, size - 1 : size], (heads, size))
        decays = jnp.exp2(last)
        tails = jnp.exp2(last - shift)
        start_ref[c] = jnp.exp2(past)
        for g in range(count):
            scores = lax.dot_general(
                c_ref[c, g], b_ref[c, g], (((1,), (1,)), ((), ())), preferred_element_type=F32
            )
            scores_ref[c, g] = jnp.where(causal, scores, 0.0)
            turned = jnp.transpose(b_ref[c, g].astype(F32))
            for k in range(0, per_group, 2):
                pair = range(g * per_group + k, g * per_group + k + 2)
                delta = paired([turned * tails[h : h + 1, :] for h in pair], [x_ref[c, h] for h in pair])
                for j, h in enumerate(pair):
                    states[c + 1, h] = (
                        decays[h : h + 1, :] * states[c, h]
                        + delta[:, j * head_size : (j + 1) * head_size]
                    )
        columns = jnp.transpose(cumul)
        for h in range(heads):
            along = jnp.broadcast_to(columns[:, h : h + 1], (size, size))
            y_ref[c, h] = along
            grow_ref[c, h] = jnp.exp2(along)
        for j in range(each):
            enter[0, jnp.minimum(c * each, heads - each) + j] = jnp.transpose(hist_ref[c, j])
        return past + last

    total[...] = jnp.exp2(lax.fori_loop(0, blocks // GATHER, gather_some, jnp.zeros((heads, size), F32)))
    first = jnp.where(me == 0, total[...], 0.0)

    for h in range(heads):
        send[h] = first[h : h + 1, :] * enter[0, h] + states[blocks, h]
    pl.semaphore_wait(barrier, peers - 1)

    def swap(g):
        span = pl.ds(g * per_group, per_group)
        return pltpu.make_async_remote_copy(
            src_ref=send.at[span], dst_ref=enter.at[1, span],
            send_sem=send_sem.at[g], recv_sem=recv_sem.at[g], **peer(1 - me),
        )

    def swap_total():
        return pltpu.make_async_remote_copy(
            src_ref=total, dst_ref=their_total,
            send_sem=fin_send_sem.at[0, 0], recv_sem=fin_recv_sem.at[0], **peer(1 - me),
        )

    def link(g):
        span = pl.ds(g * per_group, per_group)
        return pltpu.make_async_remote_copy(
            src_ref=send.at[span], dst_ref=enter.at[1, span],
            send_sem=send_sem.at[g], recv_sem=recv_sem.at[g],
            **peer(jnp.minimum(me + 1, peers - 1)),
        )

    def to_peer(d, g):
        span = pl.ds(g * per_group, per_group)
        return pltpu.make_async_remote_copy(
            src_ref=full.at[d, span], dst_ref=fin_ref.at[span],
            send_sem=fin_send_sem.at[d, g], recv_sem=fin_recv_sem.at[g],
            **peer(d),
        )

    if peers == 2:
        for g in range(count):
            swap(g).start()
        swap_total().start()
    else:

        @pl.when(me == 0)
        def _():
            for g in range(count):
                link(g).start()

    def within(c, carry):
        shift = shift_ref[c]
        for g in range(count):
            scores = scores_ref[c, g]
            for k in range(0, per_group, 2):
                pair = range(g * per_group + k, g * per_group + k + 2)
                y = paired(
                    [
                        scores * jnp.exp2(jnp.minimum(y_ref[c, h] - shift[h : h + 1, :], 0.0))
                        + skips_ref[h]
                        for h in pair
                    ],
                    [x_ref[c, h] for h in pair],
                )
                for j, h in enumerate(pair):
                    y_ref[c, h] = y[:, j * head_size : (j + 1) * head_size]
        return carry

    middle = blocks if peers == 2 else (blocks + 1) // 2
    lax.fori_loop(0, middle, within, 0, unroll=WITHIN)

    if peers == 2:
        for g in range(count):
            swap(g).wait()
        swap_total().wait()
        coef_ref[0] = jnp.where(me == 0, their_total[...], one)
        coef_ref[1] = jnp.where(me == 0, one, total[...])
    else:

        @pl.when(me > 0)
        def _():
            for g in range(count):
                link(g).wait_recv()
                for h in range(g * per_group, (g + 1) * per_group):
                    send[h] = total[h : h + 1, :] * enter[1, h] + states[blocks, h]

                @pl.when(me < peers - 1)
                def _(g=g):
                    link(g).start()

                @pl.when(me == peers - 1)
                def _(g=g):
                    for h in range(g * per_group, (g + 1) * per_group):
                        closing = jnp.transpose(send[h])
                        for d in range(peers - 1):
                            full[d, h] = closing[d * share : (d + 1) * share]
                        fin_ref[h] = closing[(peers - 1) * share :]
                    for d in range(peers - 1):
                        to_peer(d, g).start()

        coef_ref[...] = jnp.zeros_like(coef_ref)
        lax.fori_loop(middle, blocks, within, 0)

    def last_fetched(c, carry):
        fetched(z_ref, z_sem, c)
        return carry

    lax.fori_loop(0, blocks, last_fetched, 0)

    if peers == 2:
        fin_ref[...] = jnp.zeros_like(fin_ref)
    else:

        @pl.when(me == peers - 1)
        def _():
            for g in range(count):
                for d in range(peers - 1):
                    to_peer(d, g).wait_send()

        @pl.when(me < peers - 1)
        def _():
            for g in range(count):
                link(g).wait_send()
            for g in range(count):
                to_peer(0, g).wait_recv()


def mix_kernel(
    peers, gain_ref, states, enter, send, coef_ref, fin_ref, y_ref, z_ref, c_ref, grow_ref, start_ref,
    out_hbm, fin_hbm, gated, turned, out_ref, out_sem, fin_sem,
):
    blocks, heads, size, head_size = y_ref.shape
    count, width = c_ref.shape[1], c_ref.shape[3]
    per_group = heads // count
    share = head_size // peers
    each = -(-heads // blocks)

    me = lax.axis_index("seq")
    source = jnp.minimum(me, 1)

    if peers == 2:

        def fin_copy(c):
            span = pl.ds(jnp.minimum(c * each, heads - each), each)
            mine = pl.ds(pl.multiple_of(me * share, share), share)
            return pltpu.make_async_copy(turned.at[c, :, mine], fin_hbm.at[span], fin_sem.at[c])
    else:

        whole_copy = pltpu.make_async_copy(fin_ref, fin_hbm, fin_sem.at[0])
        whole_copy.start()

    eye = (
        lax.broadcasted_iota(jnp.int32, (head_size, head_size), 0)
        == lax.broadcasted_iota(jnp.int32, (head_size, head_size), 1)
    ).astype(F32).astype(BF16)

    def block(c, carry):
        starts = start_ref[c]
        if peers == 2:
            for j in range(each):
                h = jnp.minimum(c * each, heads - each) + j
                turned[c, j] = jnp.transpose(
                    coef_ref[0, pl.ds(h, 1), :] * send[h]
                    + coef_ref[1, pl.ds(h, 1), :] * enter[1, h]
                )
        for g in range(count):
            read = c_ref[c, g]
            left = jnp.concatenate([read, read], axis=1)
            squares = jnp.zeros((size, head_size), F32)
            for k in range(0, per_group, 2):
                pair = range(g * per_group + k, g * per_group + k + 2)
                right = [
                    jnp.concatenate(
                        split(states[c, h] + starts[h : h + 1, :] * enter[source, h]), axis=0
                    )
                    for h in pair
                ]
                earlier = jnp.dot(
                    left, jnp.concatenate(right, axis=1), preferred_element_type=F32
                )
                for j, h in enumerate(pair):
                    along = grow_ref[c, h]
                    y = y_ref[c, h] + along * earlier[:, j * head_size : (j + 1) * head_size]
                    z = z_ref[c, h].astype(F32)
                    if j == 0:
                        z = jnp.dot(z_ref[c, h], eye, preferred_element_type=F32)
                    value = y * (z * jax.nn.sigmoid(z))
                    gated[h - g * per_group] = value
                    squares = squares + value * value
            mean = jnp.sum(squares, axis=1, keepdims=True) * (1.0 / (per_group * head_size))
            scale = jnp.broadcast_to(lax.rsqrt(mean + 1e-05), (size, head_size))
            for k in range(per_group):
                h = g * per_group + k
                gain = gain_ref[pl.ds(h * head_size, head_size)].astype(F32).reshape(1, head_size)
                out_ref[c, h] = (gated[k] * scale * gain).astype(BF16)
                pltpu.make_async_copy(
                    out_ref.at[c, h],
                    out_hbm.at[pl.ds(c * size, size), pl.ds(h * head_size, head_size)],
                    out_sem.at[c],
                ).start()
        if peers == 2:
            fin_copy(c).start()
        return carry

    lax.fori_loop(0, blocks, block, 0, unroll=2)

    def sent(c, carry):
        pltpu.make_async_copy(out_ref.at[c], out_ref.at[c], out_sem.at[c]).wait()
        if peers == 2:
            fin_copy(c).wait()
        return carry

    lax.fori_loop(0, blocks, sent, 0)
    if peers > 2:
        whole_copy.wait()


def body(
    values, gate_in, write_proj, read_proj, step_size, log_gate, skip_gain, norm_gain, history
):
    heads, head_size, width = history.shape
    groups = write_proj.shape[1] // width
    rows = values.shape[0]
    peers = lax.axis_size("seq")
    share = head_size // peers
    size = math.gcd(rows, 128)
    blocks = rows // size
    in_vmem = pl.BlockSpec(memory_space=pltpu.VMEM)
    in_hbm = pl.BlockSpec(memory_space=pltpu.HBM)
    dma = pltpu.SemaphoreType.DMA
    relay = heads if peers > 2 else 1
    each = -(-heads // blocks)

    handed = pl.pallas_call(
        functools.partial(chain_kernel, peers),
        in_specs=[in_hbm] * 8,
        out_specs=[in_vmem] * 10,
        out_shape=[
            pltpu.VMEM((blocks + 1, heads, width, head_size), F32),
            pltpu.VMEM((2, heads, width, head_size), F32),
            pltpu.VMEM((heads, width, head_size), F32),
            pltpu.VMEM((2, heads, size), F32),
            pltpu.VMEM((heads if peers > 2 else 1, share, width), F32),
            pltpu.VMEM((blocks, heads, size, head_size), F32),
            pltpu.VMEM((blocks, heads, size, head_size), BF16),
            pltpu.VMEM((blocks, groups, size, width), BF16),
            pltpu.VMEM((blocks, heads, size, head_size), F32),
            pltpu.VMEM((blocks, heads, size), F32),
        ],
        scratch_shapes=[
            pltpu.VMEM((blocks, heads, size, head_size), BF16),
            pltpu.VMEM((blocks, groups, size, width), BF16),
            pltpu.VMEM((heads, rows), F32),
            pltpu.VMEM((heads, rows), F32),
            pltpu.VMEM((blocks, each, head_size, width), F32),
            pltpu.SMEM((heads,), F32),
            pltpu.VMEM((blocks, heads, size), F32),
            pltpu.VMEM((blocks, heads, size), F32),
            pltpu.VMEM((blocks, groups, size, size), F32),
            pltpu.VMEM((heads, size, size), F32),
            pltpu.VMEM((heads, size), F32),
            pltpu.VMEM((heads, size), F32),
            pltpu.VMEM((peers - 1, relay, share, width), F32),
            dma((blocks,)),
            dma((blocks,)),
            dma((blocks,)),
            dma((blocks,)),
            dma((blocks,)),
            dma((3,)),
            dma((groups,)),
            dma((groups,)),
            dma((peers - 1, groups)),
            dma((groups,)),
        ],
        compiler_params=pltpu.CompilerParams(
            collective_id=0, has_side_effects=True, vmem_limit_bytes=VMEM
        ),
        name="chain",
    )(
        *(
            pltpu.with_memory_space_constraint(array, pltpu.HBM)
            for array in (
                values, gate_in, write_proj, read_proj, step_size.T, log_gate.T, history,
                skip_gain,
            )
        )
    )

    normed, final_state = pl.pallas_call(
        functools.partial(mix_kernel, peers),
        in_specs=[in_vmem] * 11,
        out_specs=[in_hbm] * 2,
        out_shape=[
            jax.ShapeDtypeStruct((rows, heads * head_size), BF16),
            jax.ShapeDtypeStruct((heads, share, width), F32),
        ],
        scratch_shapes=[
            pltpu.VMEM((heads // groups, size, head_size), F32),
            pltpu.VMEM((blocks, each, head_size, width), F32),
            pltpu.VMEM((blocks, heads, size, head_size), BF16),
            dma((blocks,)),
            dma((blocks,)),
        ],
        compiler_params=pltpu.CompilerParams(vmem_limit_bytes=VMEM),
        name="mix",
    )(norm_gain, *handed)
    return normed, final_state


def solution(mesh):
    rows = P(("batch", "seq"), "tp")
    return jax.shard_map(
        body,
        mesh=mesh,
        in_specs=(rows, rows, rows, rows, rows, rows, P("tp"), P("tp"), P(("batch", "tp"), None, None)),
        out_specs=(rows, P(("batch", "tp"), "seq", None)),
        check_vma=False,
    )
```
